256 devices in a mesh: dp: 32 (over y, x, z_lo), mp: 8 (over z_hi, core).
Axes of the slice: x: 4, y: 4, z: 8 (z_hi: 4, z_lo: 2; z = z_hi * 2 + z_lo), core: 2. Of those that a mesh axis runs over, the one named last changes fastest.
Arguments:
- inputs: bfloat16 [4096, 16384], P('dp', 'mp'), may hold values from -6 to 6
- projector: bfloat16 [16384, 1024], P('dp', 'mp'), may hold values from -0.046875 to 0.046875
- out_grads: bfloat16 [4096, 26624], P('dp', 'mp'), may hold values from -0.25 to 0.25
- weights: bfloat16 [16384, 26624], P('dp', 'mp'), may hold values from -6 to 6
- first_moment: float32 [1024, 26624], P('dp', 'mp'), may hold values from -1.5 to 1.5
- second_moment: float32 [1024, 26624], P('dp', 'mp'), may hold values from 0.01 to 1
Outputs:
- new_weights: bfloat16 [16384, 26624], P('dp', 'mp')
- new_first: float32 [1024, 26624], P('dp', 'mp')
- new_second: float32 [1024, 26624], P('dp', 'mp')
The draws below stay inside these ranges and needn't reach their ends.
All inputs are finite; a program needn't handle non-finite values.
Results may differ from the reference program's by a relative error of at most 0.0031.
Values may be sent and summed in bfloat16 or wider, within the bound.
A program may use at most 128 MiB of HBM per device.

```python
import math
import jax
import jax.numpy as jnp
from jax import lax

D = 16384
FF = 26624
RANK = 1024
STEP = 1000
TOKENS = 4096


def shard_levels(rng, dims, shards, smallest, high):
    factor_of, own = 1.0, jax.random.fold_in(rng, 6)
    for axis_at, shards_of in shards:
        steps = jnp.exp(jax.random.uniform(jax.random.fold_in(own, axis_at), (shards_of,), jnp.float32, smallest / len(shards), high / len(shards)))
        factor_of = factor_of * jnp.repeat(steps, dims[axis_at] // shards_of).reshape([-1 if axis == axis_at else 1 for axis in range(len(dims))])
    return factor_of


def noise(stream_key, extent, deviation, bound, split=(), dtype=jnp.bfloat16):
    gain = shard_levels(stream_key, extent, split, -0.22, 0.18) if split else 1.0
    drawn = jax.random.normal(stream_key, extent, jnp.float32) * deviation * gain
    return jnp.minimum(jnp.maximum(drawn, -bound), bound).astype(dtype)


def setup_inputs(seed: int = 0) -> dict:
    key_of = jax.random.split(jax.random.key(seed), 7)
    return {
        "inputs": noise(key_of[0], (TOKENS, D), 1.0, 6.0, ((0, 32), (1, 8))),
        "projector": noise(key_of[1], (D, RANK), D ** -0.5, 0.046875, ((0, 32), (1, 8))),
        "out_grads": noise(key_of[2], (TOKENS, FF), (TOKENS ** -0.5), 0.25, ((0, 32), (1, 8))),
        "weights": noise(key_of[3], (D, FF), 1.0, 6.0, ((0, 32), (1, 8))),
        "first_moment": noise(key_of[4], (RANK, FF), 0.1, 1.5, ((0, 32), (1, 8)), jnp.float32),
        "second_moment": jnp.clip(jnp.exp(math.log(1.0) - 4.6051702 * jax.random.uniform(key_of[5], (RANK, FF), jnp.float32) ** shard_levels(key_of[5], (RANK, FF), ((0, 32), (1, 8)), -0.2, 0.2)), 0.01, 1.0),
    }


def reference(inputs, projector, out_grads, weights, first_moment, second_moment):
    projected = jnp.dot(inputs, projector, preferred_element_type=jnp.float32).astype(jnp.bfloat16)
    compressed = lax.dot_general(projected, out_grads, (((0,), (0,)), ((), ())), preferred_element_type=jnp.float32)
    new_first = 0.9 * first_moment + 0.1 * compressed
    new_second = 0.999 * second_moment + 0.001 * compressed * compressed
    first_fix = 1.0 - 0.9 ** STEP
    second_fix = 1.0 - 0.999 ** STEP
    direction = (new_first / first_fix / (jnp.sqrt(new_second / second_fix) + 1e-08)).astype(jnp.bfloat16)
    blocks = D // 16
    proj_blocks = projector.reshape(16, blocks, RANK)
    weight_blocks = weights.reshape(16, blocks, FF)

    def lift_block(pair):
        proj_part, weight_part = pair
        lifted = jnp.dot(proj_part, direction, preferred_element_type=jnp.float32)
        return (weight_part.astype(jnp.float32) - 2.0 * lifted).astype(jnp.bfloat16)
    new_weights = lax.map(lift_block, (proj_blocks, weight_blocks)).reshape(D, FF)
    return (new_weights, new_first, new_second)
```

```python
import jax
import jax.numpy as jnp
from jax import lax
from jax.experimental import pallas as pl
from jax.experimental.pallas import tpu as pltpu
from jax.sharding import Mesh
from jax.sharding import PartitionSpec as P

STEP = 1000
AXES = ("dp_0", "dp_1", "dp_2", "mp_0", "mp_1")
DP = AXES[:3]
MP = AXES[3:]
MESH = pl.DeviceIdType.MESH
ANY = pl.BlockSpec(memory_space=pl.ANY)
VMEM = pl.BlockSpec(memory_space=pltpu.VMEM)
DMA = pltpu.SemaphoreType.DMA


def place():
    return tuple(lax.axis_index(a) for a in AXES)


def remote(src, dst, send_sem, recv_sem, **where):
    return pltpu.make_async_remote_copy(
        src_ref=src,
        dst_ref=dst,
        send_sem=send_sem,
        recv_sem=recv_sem,
        device_id=where,
        device_id_type=MESH,
    )


def landed(dst, sem):
    pltpu.make_async_copy(dst, dst, sem).wait()


def rows(start, size, unit=None):
    return pl.ds(pl.multiple_of(start, unit or size), size)


def greet(peers, extra=None):
    barrier = pltpu.get_barrier_semaphore()
    for peer in peers:
        pl.semaphore_signal(barrier, inc=1, device_id=peer, device_id_type=MESH)
    count = len(peers)
    if extra is not None:
        peer, present = extra

        @pl.when(present)
        def _():
            pl.semaphore_signal(barrier, inc=1, device_id=peer, device_id_type=MESH)

        count = count + present.astype(jnp.int32)
    pl.semaphore_wait(barrier, count)


def projected_kernel(
    inp, proj, grads, pa, g4,
    inp4, pt, pq, part, half_in, rs_in, g_own,
    loc_sem, inp_s, inp_r, g_s, g_r, pt_s, pt_r, pq_s, pq_r, half_s, half_r, rs_s, rs_r, pa_s, pa_r,
):
    y, x, zl, h, c = place()
    up, down = lax.rem(y + 1, 4), lax.rem(y + 3, 4)
    tok = inp.shape[0]
    half = tok // 2
    feat = proj.shape[0]
    lanes = proj.shape[1]
    peers = [{"dp_0": up}, {"dp_0": down}]
    for dx in range(4):
        for dz in range(2):
            for dc in range(2):
                if dx or dz or dc:
                    peers.append({
                        "dp_1": lax.rem(x + dx, 4),
                        "dp_2": lax.rem(zl + dz, 2),
                        "mp_1": lax.rem(c + dc, 2),
                    })
    for dh in range(1, 4):
        for dc in range(2):
            peers.append({"mp_0": lax.rem(h + dh, 4), "mp_1": lax.rem(c + dc, 2)})
    greet(peers, ({"dp_0": h, "mp_0": y}, y != h))

    in_up = remote(inp, inp4.at[1], inp_s.at[0], inp_r.at[0], dp_0=up)
    in_dn = remote(inp, inp4.at[3], inp_s.at[1], inp_r.at[1], dp_0=down)
    swap = remote(proj, pt, pt_s.at[0], pt_r.at[0], dp_0=h, mp_0=y)
    swap_here = pltpu.make_async_copy(proj, pt, pt_r.at[0])

    @pl.when(y != h)
    def _():
        swap.start()

    @pl.when(y == h)
    def _():
        swap_here.start()

    in_up.start()
    in_dn.start()
    own_in = pltpu.make_async_copy(inp, inp4.at[0], loc_sem.at[0])
    own_in.start()
    own_g = pltpu.make_async_copy(grads, g_own, loc_sem.at[1])
    own_g.start()

    landed(pt, pt_r.at[0])
    core = x // 2
    spot = pq.at[rows((lax.rem(x, 2) * 2 + zl) * feat, feat), rows(c * lanes, lanes)]
    mark = (lax.rem(x, 2) * 2 + zl) * 2 + c
    spread = []
    for dx in (1, 3, 2, 0):
        for dz in (1, 0):
            if dx or dz:
                cp = remote(
                    pt, spot, pq_s.at[dx * 2 + dz], pq_r.at[mark],
                    dp_1=lax.rem(x + dx, 4), dp_2=lax.rem(zl + dz, 2), mp_1=core,
                )
                cp.start()
                spread.append(cp)
    other = remote(pt, spot, pq_s.at[0], pq_r.at[mark], mp_1=1 - c)
    here = pltpu.make_async_copy(pt, spot, pq_r.at[mark])

    @pl.when(core != c)
    def _():
        other.start()

    @pl.when(core == c)
    def _():
        here.start()

    in_up.wait_recv()
    fw_up = remote(
        inp4.at[1, pl.ds(0, half)], inp4.at[2, pl.ds(0, half)], inp_s.at[2], inp_r.at[2], dp_0=up
    )
    fw_up.start()
    in_dn.wait_recv()
    fw_dn = remote(
        inp4.at[3, pl.ds(half, half)], inp4.at[2, pl.ds(half, half)], inp_s.at[3], inp_r.at[3], dp_0=down
    )
    fw_dn.start()
    g_up = remote(grads, g4.at[pl.ds(tok, tok)], g_s.at[0], g_r.at[0], dp_0=up)
    g_dn = remote(grads, g4.at[pl.ds(3 * tok, tok)], g_s.at[1], g_r.at[1], dp_0=down)
    g_up.start()
    g_dn.start()
    own_g.wait()
    put_g = pltpu.make_async_copy(g_own, g4.at[pl.ds(0, tok)], loc_sem.at[2])
    put_g.start()

    own_in.wait()
    for k in range(8):
        landed(pq.at[pl.ds((k // 2) * feat, feat), pl.ds((k % 2) * lanes, lanes)], pq_r.at[k])
    for b in (0, 1, 3):
        part[pl.ds(b * tok, tok)] = jnp.dot(inp4[b], pq[...], preferred_element_type=jnp.float32)
    fw_up.wait_recv()
    fw_dn.wait_recv()
    part[pl.ds(2 * tok, tok)] = jnp.dot(inp4[2], pq[...], preferred_element_type=jnp.float32)

    many = 2 * tok
    pair = remote(part.at[rows((1 - c) * many, many)], half_in, half_s.at[0], half_r.at[0], mp_1=1 - c)
    pair.start()
    pair.wait()
    mine = rows(c * many, many)
    part[mine] += half_in[...]
    cut = many // 4
    sums = []
    for dh in range(1, 4):
        to = lax.rem(h + dh, 4)
        cp = remote(
            part.at[rows(c * many + to * cut, cut)], rs_in.at[dh - 1], rs_s.at[dh - 1], rs_r.at[dh - 1], mp_0=to
        )
        cp.start()
        sums.append(cp)
    for cp in sums:
        cp.wait_recv()
    piece = rows(c * many + h * cut, cut)
    pa[piece] = (part[piece] + rs_in[0] + rs_in[1] + rs_in[2]).astype(pa.dtype)
    shares = []
    for dh in range(4):
        for dc in range(2):
            if dh or dc:
                k = dh * 2 + dc - 1
                cp = remote(
                    pa.at[piece], pa.at[piece], pa_s.at[k], pa_r.at[k],
                    mp_0=lax.rem(h + dh, 4), mp_1=lax.rem(c + dc, 2),
                )
                cp.start()
                shares.append(cp)

    g_up.wait_recv()
    gf_up = remote(
        g4.at[pl.ds(tok, half)], g4.at[pl.ds(2 * tok, half)], g_s.at[2], g_r.at[2], dp_0=up
    )
    gf_up.start()
    g_dn.wait_recv()
    gf_dn = remote(
        g4.at[pl.ds(3 * tok + half, half)], g4.at[pl.ds(2 * tok + half, half)], g_s.at[3], g_r.at[3], dp_0=down
    )
    gf_dn.start()

    for k in range(1, 8):
        frm_h, frm_c = lax.rem(h + 4 - k // 2, 4), lax.rem(c + 2 - k % 2, 2)
        landed(pa.at[rows(frm_c * many + frm_h * cut, cut)], pa_r.at[k - 1])
    gf_up.wait_recv()
    gf_dn.wait_recv()
    put_g.wait()
    for cp in (in_up, in_dn, fw_up, fw_dn, g_up, g_dn, gf_up, gf_dn, *spread, *sums, *shares):
        cp.wait_send()

    @pl.when(y != h)
    def _():
        swap.wait_send()

    @pl.when(core != c)
    def _():
        other.wait_send()


def gather_projected(inputs, projector, out_grads):
    tok, feats = inputs.shape
    feat, lanes = projector.shape
    cols = out_grads.shape[1]
    bf, f32 = jnp.bfloat16, jnp.float32
    return pl.pallas_call(
        projected_kernel,
        name="gather_projected",
        out_shape=(
            jax.ShapeDtypeStruct((4 * tok, 2 * lanes), bf),
            jax.ShapeDtypeStruct((4 * tok, cols), bf),
        ),
        in_specs=[ANY] * 3,
        out_specs=(VMEM, ANY),
        scratch_shapes=[
            pltpu.VMEM((4, tok, feats), bf),
            pltpu.VMEM((feat, lanes), bf),
            pltpu.VMEM((4 * feat, 2 * lanes), bf),
            pltpu.VMEM((4 * tok, 2 * lanes), f32),
            pltpu.VMEM((2 * tok, 2 * lanes), f32),
            pltpu.VMEM((3, tok // 2, 2 * lanes), f32),
            pltpu.VMEM((tok, cols), bf),
            DMA((3,)),
            DMA((4,)), DMA((4,)),
            DMA((4,)), DMA((4,)),
            DMA((1,)), DMA((1,)),
            DMA((8,)), DMA((8,)),
            DMA((1,)), DMA((1,)),
            DMA((3,)), DMA((3,)),
            DMA((7,)), DMA((7,)),
        ],
        compiler_params=pltpu.CompilerParams(collective_id=0, has_side_effects=True),
    )(inputs, projector, out_grads)


def reduce_kernel(
    part, out, raw_l, raw_r, via_l, via_r, turn_r, turn_l, add_l, add_r, zsend, zrecv,
    s_sem, r_sem,
):
    y, x, zl, h, c = place()
    right, left, far = lax.rem(x + 1, 4), lax.rem(x + 3, 4), lax.rem(x + 2, 4)
    n = out.shape[0]
    f32 = jnp.float32
    greet([{"dp_1": right}, {"dp_1": left}, {"dp_2": 1 - zl}])

    def piece(of, half):
        return part.at[rows(of * 2 * n + half * n, n)]

    far_r = remote(piece(far, 0), via_l, s_sem.at[0], r_sem.at[0], dp_1=right)
    far_l = remote(piece(far, 1), via_r, s_sem.at[1], r_sem.at[1], dp_1=left)
    near_r = remote(piece(right, 1), raw_l, s_sem.at[2], r_sem.at[2], dp_1=right)
    near_l = remote(piece(left, 0), raw_r, s_sem.at[3], r_sem.at[3], dp_1=left)
    far_r.start()
    far_l.start()
    near_r.start()
    near_l.start()
    far_r.wait_recv()
    turn_r[...] = (via_l[...].astype(f32) + part[rows(right * 2 * n, n)].astype(f32)).astype(turn_r.dtype)
    on_r = remote(turn_r, add_l, s_sem.at[4], r_sem.at[4], dp_1=right)
    on_r.start()
    far_l.wait_recv()
    turn_l[...] = (via_r[...].astype(f32) + part[rows(left * 2 * n + n, n)].astype(f32)).astype(turn_l.dtype)
    on_l = remote(turn_l, add_r, s_sem.at[5], r_sem.at[5], dp_1=left)
    on_l.start()
    near_r.wait_recv()
    near_l.wait_recv()
    on_r.wait_recv()
    on_l.wait_recv()

    def total(first):
        if first:
            return part[rows(x * 2 * n, n)].astype(f32) + add_l[...].astype(f32) + raw_r[...].astype(f32)
        return part[rows(x * 2 * n + n, n)].astype(f32) + add_r[...].astype(f32) + raw_l[...].astype(f32)

    @pl.when(zl == 0)
    def _():
        zsend[...] = total(False).astype(zsend.dtype)

    @pl.when(zl == 1)
    def _():
        zsend[...] = total(True).astype(zsend.dtype)

    swap = remote(zsend, zrecv, s_sem.at[6], r_sem.at[6], dp_2=1 - zl)
    swap.start()

    @pl.when(zl == 0)
    def _():
        out[...] = total(True)

    @pl.when(zl == 1)
    def _():
        out[...] = total(False)

    swap.wait_recv()
    out[...] += zrecv[...].astype(f32)
    for cp in (far_r, far_l, near_r, near_l, on_r, on_l, swap):
        cp.wait_send()


def reduce_rows(part):
    n, cols = part.shape[0] // 8, part.shape[1]
    slot = pltpu.VMEM((n, cols), part.dtype)
    return pl.pallas_call(
        reduce_kernel,
        name="reduce_rows",
        out_shape=jax.ShapeDtypeStruct((n, cols), jnp.float32),
        in_specs=[VMEM],
        out_specs=VMEM,
        scratch_shapes=[slot] * 10 + [DMA((7,)), DMA((7,))],
        compiler_params=pltpu.CompilerParams(collective_id=1, has_side_effects=True),
    )(part)


def spread_kernel(own, proj, full, prow, stage, loc_sem, z_s, z_r, a_s, a_r, b_s, b_r, p_s, p_r):
    y, x, zl, h, c = place()
    n, cols = own.shape
    lanes = proj.shape[1]
    wide = cols // 2
    rank = (y * 4 + x) * 2 * n
    pair = lax.rem(x + 2, 4)
    peers = [{"dp_2": 1 - zl}]
    for axis, at in (("dp_0", y), ("dp_1", x)):
        peers += [{axis: lax.rem(at + 1, 4)}, {axis: lax.rem(at + 3, 4)}]
    for dh in range(4):
        for dc in range(2):
            if dh or dc:
                if dh == 0:
                    peers.append({"mp_1": 1 - c})
                else:
                    peers.append({"mp_0": lax.rem(h + dh, 4), "mp_1": lax.rem(c + dc, 2)})
    greet(peers)

    mine = full.at[rows(rank + zl * n, n)]
    z = remote(own, mine, z_s, z_r, dp_2=1 - zl)
    z.start()
    put = pltpu.make_async_copy(own, mine, loc_sem.at[0])
    put.start()
    take = pltpu.make_async_copy(proj, stage, loc_sem.at[1])
    take.start()
    put.wait()
    landed(full.at[rows(rank + (1 - zl) * n, n)], z_r)
    take.wait()
    here = prow.at[:, rows((h * 2 + c) * lanes, lanes)]
    keep = pltpu.make_async_copy(stage, here, loc_sem.at[2])
    keep.start()

    sent = []
    todo = []
    colours = []
    for col, s, r, first, second in ((0, a_s, a_r, "dp_1", "dp_0"), (1, b_s, b_r, "dp_0", "dp_1")):
        at1 = x if first == "dp_1" else y
        at2 = y if first == "dp_1" else x
        f1 = 1 if first == "dp_1" else 4
        f2 = 4 if first == "dp_1" else 1

        def region(p1, p2, start, size, col=col, f1=f1, f2=f2):
            return full.at[rows((p1 * f1 + p2 * f2) * 2 * n + start, size, n), pl.ds(col * wide, wide)]

        colours.append((s, r, first, second, at1, at2, region))

    def send(colour, k, axis, to, where):
        s, r = colour[0], colour[1]
        cp = remote(where, where, s.at[k], r.at[k], **{axis: to})
        cp.start()
        sent.append(cp)

    def plus(at, d):
        return lax.rem(at + d, 4)

    for col in colours:
        s, r, first, second, at1, at2, region = col
        send(col, 0, first, plus(at1, 1), region(at1, at2, 0, 2 * n))
        send(col, 1, first, plus(at1, 3), region(at1, at2, 0, 2 * n))
    ahead = []
    for col in colours:
        s, r, first, second, at1, at2, region = col
        landed(region(plus(at1, 3), at2, 0, 2 * n), r.at[0])
        send(col, 2, first, plus(at1, 1), region(plus(at1, 3), at2, 0, n))
        landed(region(plus(at1, 1), at2, 0, 2 * n), r.at[1])
        send(col, 3, first, plus(at1, 3), region(plus(at1, 1), at2, n, n))
    for col in colours:
        s, r, first, second, at1, at2, region = col
        for i, d in enumerate((0, 3, 1)):
            send(col, 4 + i, second, plus(at2, 1), region(plus(at1, d), at2, 0, 2 * n))
            send(col, 8 + i, second, plus(at2, 3), region(plus(at1, d), at2, 0, 2 * n))
    k = 0
    for dh in range(4):
        for dc in range(2):
            if dh or dc:
                where = (
                    {"mp_1": 1 - c} if dh == 0
                    else {"mp_0": lax.rem(h + dh, 4), "mp_1": lax.rem(c + dc, 2)}
                )
                cp = remote(stage, here, p_s.at[k], p_r.at[k], **where)
                cp.start()
                sent.append(cp)
                k += 1
    for col in colours:
        s, r, first, second, at1, at2, region = col
        landed(region(plus(at1, 2), at2, 0, n), r.at[2])
        landed(region(plus(at1, 2), at2, n, n), r.at[3])
        send(col, 7, second, plus(at2, 1), region(plus(at1, 2), at2, 0, 2 * n))
        send(col, 11, second, plus(at2, 3), region(plus(at1, 2), at2, 0, 2 * n))
    for i, d in enumerate((0, 3, 1, 2)):
        for col in colours:
            s, r, first, second, at1, at2, region = col
            landed(region(plus(at1, d), plus(at2, 3), 0, 2 * n), r.at[4 + i])
            send(col, 12 + i, second, plus(at2, 1), region(plus(at1, d), plus(at2, 3), 0, n))
            landed(region(plus(at1, d), plus(at2, 1), 0, 2 * n), r.at[8 + i])
            send(col, 16 + i, second, plus(at2, 3), region(plus(at1, d), plus(at2, 1), n, n))
    for i, d in enumerate((0, 3, 1, 2)):
        for col in colours:
            s, r, first, second, at1, at2, region = col
            landed(region(plus(at1, d), plus(at2, 2), 0, n), r.at[12 + i])
            landed(region(plus(at1, d), plus(at2, 2), n, n), r.at[16 + i])
    k = 0
    for dh in range(4):
        for dc in range(2):
            if dh or dc:
                frm = lax.rem(h + 4 - dh, 4) * 2 + lax.rem(c + 2 - dc, 2)
                landed(prow.at[:, rows(frm * lanes, lanes)], p_r.at[k])
                k += 1
    keep.wait()
    z.wait_send()
    for cp in sent:
        cp.wait_send()


def spread_direction(direction, projector):
    n, cols = direction.shape
    feat, lanes = projector.shape
    bf = jnp.bfloat16
    return pl.pallas_call(
        spread_kernel,
        name="spread_direction",
        out_shape=(
            jax.ShapeDtypeStruct((32 * n, cols), bf),
            jax.ShapeDtypeStruct((feat, 8 * lanes), bf),
        ),
        in_specs=[VMEM, ANY],
        out_specs=(ANY, ANY),
        scratch_shapes=[
            pltpu.VMEM((feat, lanes), bf),
            DMA((3,)),
            DMA, DMA,
            DMA((20,)), DMA((20,)),
            DMA((20,)), DMA((20,)),
            DMA((7,)), DMA((7,)),
        ],
        compiler_params=pltpu.CompilerParams(collective_id=2, has_side_effects=True),
    )(direction, projector)


def per_device(inputs, projector, out_grads, weights, first_moment, second_moment):
    projected, grads = gather_projected(inputs, projector, out_grads)
    part = lax.dot_general(
        projected, grads, (((0,), (0,)), ((), ())), preferred_element_type=jnp.float32
    ).astype(jnp.bfloat16)
    compressed = reduce_rows(part)
    new_first = 0.9 * first_moment + 0.1 * compressed
    new_second = 0.999 * second_moment + 0.001 * compressed * compressed
    first_fix = 1.0 - 0.9**STEP
    second_fix = 1.0 - 0.999**STEP
    direction = (new_first / first_fix / (jnp.sqrt(new_second / second_fix) + 1e-08)).astype(
        jnp.bfloat16
    )
    full, ranks = spread_direction(direction, projector)
    lifted = jnp.dot(ranks, full, preferred_element_type=jnp.float32)
    new_weights = (weights.astype(jnp.float32) - 2.0 * lifted).astype(jnp.bfloat16)
    return (new_weights, new_first, new_second)


def solution(mesh):
    finer = Mesh(mesh.devices.reshape(4, 4, 2, 4, 2), AXES)
    spec = P(DP, MP)
    return jax.shard_map(
        per_device, mesh=finer, in_specs=(spec,) * 6, out_specs=(spec,) * 3, check_vma=False
    )
```

```python
import functools

import jax
import jax.numpy as jnp
from jax import lax
from jax.experimental import pallas as pl
from jax.experimental.pallas import tpu as pltpu
from jax.sharding import Mesh
from jax.sharding import PartitionSpec as P

STEP = 1000
AXES = ("dp_0", "dp_1", "dp_2", "mp_0", "mp_1")
DP = AXES[:3]
MP = AXES[3:]
MESH = pl.DeviceIdType.MESH
ANY = pl.BlockSpec(memory_space=pl.ANY)
VMEM = pl.BlockSpec(memory_space=pltpu.VMEM)
DMA = pltpu.SemaphoreType.DMA


def place():
    return tuple(lax.axis_index(a) for a in AXES)


def remote(src, dst, send_sem, recv_sem, **where):
    return pltpu.make_async_remote_copy(
        src_ref=src,
        dst_ref=dst,
        send_sem=send_sem,
        recv_sem=recv_sem,
        device_id=where,
        device_id_type=MESH,
    )


def landed(dst, sem):
    pltpu.make_async_copy(dst, dst, sem).wait()


def rows(start, size, unit=None):
    return pl.ds(pl.multiple_of(start, unit or size), size)


def greet(peers, extra=None):
    barrier = pltpu.get_barrier_semaphore()
    for peer in peers:
        pl.semaphore_signal(barrier, inc=1, device_id=peer, device_id_type=MESH)
    count = len(peers)
    if extra is not None:
        peer, present = extra

        @pl.when(present)
        def _():
            pl.semaphore_signal(barrier, inc=1, device_id=peer, device_id_type=MESH)

        count = count + present.astype(jnp.int32)
    pl.semaphore_wait(barrier, count)


def projected_kernel(
    inp, proj, grads, pa, g4,
    inp4, pt, pq, part, half_in, rs_in, g_own,
    loc_sem, inp_s, inp_r, g_s, g_r, pt_s, pt_r, pq_s, pq_r, half_s, half_r, rs_s, rs_r, pa_s, pa_r,
):
    y, x, zl, h, c = place()
    up, down = lax.rem(y + 1, 4), lax.rem(y + 3, 4)
    tok = inp.shape[0]
    half = tok // 2
    feat = proj.shape[0]
    lanes = proj.shape[1]
    peers = [{"dp_0": up}, {"dp_0": down}]
    for dx in range(4):
        for dz in range(2):
            for dc in range(2):
                if dx or dz or dc:
                    peers.append({
                        "dp_1": lax.rem(x + dx, 4),
                        "dp_2": lax.rem(zl + dz, 2),
                        "mp_1": lax.rem(c + dc, 2),
                    })
    for dh in range(1, 4):
        for dc in range(2):
            peers.append({"mp_0": lax.rem(h + dh, 4), "mp_1": lax.rem(c + dc, 2)})
    greet(peers, ({"dp_0": h, "mp_0": y}, y != h))

    in_up = remote(inp, inp4.at[1], inp_s.at[0], inp_r.at[0], dp_0=up)
    in_dn = remote(inp, inp4.at[3], inp_s.at[1], inp_r.at[1], dp_0=down)
    swap = remote(proj, pt, pt_s.at[0], pt_r.at[0], dp_0=h, mp_0=y)
    swap_here = pltpu.make_async_copy(proj, pt, pt_r.at[0])

    @pl.when(y != h)
    def _():
        swap.start()

    @pl.when(y == h)
    def _():
        swap_here.start()

    in_up.start()
    in_dn.start()
    own_in = pltpu.make_async_copy(inp, inp4.at[0], loc_sem.at[0])
    own_in.start()
    own_g = pltpu.make_async_copy(grads, g_own, loc_sem.at[1])
    own_g.start()

    landed(pt, pt_r.at[0])
    core = x // 2
    spot = pq.at[rows((lax.rem(x, 2) * 2 + zl) * feat, feat), rows(c * lanes, lanes)]
    mark = (lax.rem(x, 2) * 2 + zl) * 2 + c
    spread = []
    for dx in (1, 3, 2, 0):
        for dz in (1, 0):
            if dx or dz:
                cp = remote(
                    pt, spot, pq_s.at[dx * 2 + dz], pq_r.at[mark],
                    dp_1=lax.rem(x + dx, 4), dp_2=lax.rem(zl + dz, 2), mp_1=core,
                )
                cp.start()
                spread.append(cp)
    other = remote(pt, spot, pq_s.at[0], pq_r.at[mark], mp_1=1 - c)
    here = pltpu.make_async_copy(pt, spot, pq_r.at[mark])

    @pl.when(core != c)
    def _():
        other.start()

    @pl.when(core == c)
    def _():
        here.start()

    in_up.wait_recv()
    fw_up = remote(
        inp4.at[1, pl.ds(0, half)], inp4.at[2, pl.ds(0, half)], inp_s.at[2], inp_r.at[2], dp_0=up
    )
    fw_up.start()
    in_dn.wait_recv()
    fw_dn = remote(
        inp4.at[3, pl.ds(half, half)], inp4.at[2, pl.ds(half, half)], inp_s.at[3], inp_r.at[3], dp_0=down
    )
    fw_dn.start()
    g_up = remote(grads, g4.at[pl.ds(tok, tok)], g_s.at[0], g_r.at[0], dp_0=up)
    g_dn = remote(grads, g4.at[pl.ds(3 * tok, tok)], g_s.at[1], g_r.at[1], dp_0=down)
    g_up.start()
    g_dn.start()
    own_g.wait()
    put_g = pltpu.make_async_copy(g_own, g4.at[pl.ds(0, tok)], loc_sem.at[2])
    put_g.start()

    own_in.wait()
    for k in range(8):
        landed(pq.at[pl.ds((k // 2) * feat, feat), pl.ds((k % 2) * lanes, lanes)], pq_r.at[k])
    for b in (0, 1, 3):
        part[pl.ds(b * tok, tok)] = jnp.dot(inp4[b], pq[...], preferred_element_type=jnp.float32)
    fw_up.wait_recv()
    fw_dn.wait_recv()
    part[pl.ds(2 * tok, tok)] = jnp.dot(inp4[2], pq[...], preferred_element_type=jnp.float32)

    many = 2 * tok
    pair = remote(part.at[rows((1 - c) * many, many)], half_in, half_s.at[0], half_r.at[0], mp_1=1 - c)
    pair.start()
    pair.wait()
    mine = rows(c * many, many)
    part[mine] += half_in[...]
    cut = many // 4
    sums = []
    for dh in range(1, 4):
        to = lax.rem(h + dh, 4)
        cp = remote(
            part.at[rows(c * many + to * cut, cut)], rs_in.at[dh - 1], rs_s.at[dh - 1], rs_r.at[dh - 1], mp_0=to
        )
        cp.start()
        sums.append(cp)
    for cp in sums:
        cp.wait_recv()
    piece = rows(c * many + h * cut, cut)
    pa[piece] = (part[piece] + rs_in[0] + rs_in[1] + rs_in[2]).astype(pa.dtype)
    shares = []
    for dh in range(4):
        for dc in range(2):
            if dh or dc:
                k = dh * 2 + dc - 1
                cp = remote(
                    pa.at[piece], pa.at[piece], pa_s.at[k], pa_r.at[k],
                    mp_0=lax.rem(h + dh, 4), mp_1=lax.rem(c + dc, 2),
                )
                cp.start()
                shares.append(cp)

    g_up.wait_recv()
    gf_up = remote(
        g4.at[pl.ds(tok, half)], g4.at[pl.ds(2 * tok, half)], g_s.at[2], g_r.at[2], dp_0=up
    )
    gf_up.start()
    g_dn.wait_recv()
    gf_dn = remote(
        g4.at[pl.ds(3 * tok + half, half)], g4.at[pl.ds(2 * tok + half, half)], g_s.at[3], g_r.at[3], dp_0=down
    )
    gf_dn.start()

    for k in range(1, 8):
        frm_h, frm_c = lax.rem(h + 4 - k // 2, 4), lax.rem(c + 2 - k % 2, 2)
        landed(pa.at[rows(frm_c * many + frm_h * cut, cut)], pa_r.at[k - 1])
    gf_up.wait_recv()
    gf_dn.wait_recv()
    put_g.wait()
    for cp in (in_up, in_dn, fw_up, fw_dn, g_up, g_dn, gf_up, gf_dn, *spread, *sums, *shares):
        cp.wait_send()

    @pl.when(y != h)
    def _():
        swap.wait_send()

    @pl.when(core != c)
    def _():
        other.wait_send()


def gather_projected(inputs, projector, out_grads):
    tok, feats = inputs.shape
    feat, lanes = projector.shape
    cols = out_grads.shape[1]
    bf, f32 = jnp.bfloat16, jnp.float32
    return pl.pallas_call(
        projected_kernel,
        name="gather_projected",
        out_shape=(
            jax.ShapeDtypeStruct((4 * tok, 2 * lanes), bf),
            jax.ShapeDtypeStruct((4 * tok, cols), bf),
        ),
        in_specs=[ANY] * 3,
        out_specs=(VMEM, ANY),
        scratch_shapes=[
            pltpu.VMEM((4, tok, feats), bf),
            pltpu.VMEM((feat, lanes), bf),
            pltpu.VMEM((4 * feat, 2 * lanes), bf),
            pltpu.VMEM((4 * tok, 2 * lanes), f32),
            pltpu.VMEM((2 * tok, 2 * lanes), f32),
            pltpu.VMEM((3, tok // 2, 2 * lanes), f32),
            pltpu.VMEM((tok, cols), bf),
            DMA((3,)),
            DMA((4,)), DMA((4,)),
            DMA((4,)), DMA((4,)),
            DMA((1,)), DMA((1,)),
            DMA((8,)), DMA((8,)),
            DMA((1,)), DMA((1,)),
            DMA((3,)), DMA((3,)),
            DMA((7,)), DMA((7,)),
        ],
        compiler_params=pltpu.CompilerParams(collective_id=0, has_side_effects=True),
    )(inputs, projector, out_grads)


def update_kernel(
    chunks, part, first_m, second_m, proj, new_first, new_second, full, prow,
    raw_l, raw_r, via_l, via_r, turn_r, turn_l, add_l, add_r, zsend, zrecv, both, stage,
    loc_sem, put_sem, rs_s, rs_r, d_s, d_r, ag_s, ag_r, p_s, p_r,
):
    y, x, zl, h, c = place()
    n = first_m.shape[0]
    lanes = proj.shape[1]
    f32 = jnp.float32
    right, left, far = lax.rem(x + 1, 4), lax.rem(x + 3, 4), lax.rem(x + 2, 4)

    def plus(at, d):
        return lax.rem(at + d, 4)

    others = []
    for dh in range(4):
        for dc in range(2):
            if dh:
                others.append({"mp_0": plus(h, dh), "mp_1": lax.rem(c + dc, 2)})
            elif dc:
                others.append({"mp_1": 1 - c})
    peers = [{"dp_2": 1 - zl}]
    for axis, at in (("dp_0", y), ("dp_1", x)):
        peers += [{axis: plus(at, 1)}, {axis: plus(at, 3)}]
    greet(peers + others)

    sent = []
    flow = {}

    def send(name, src, dst, s, r, **where):
        cp = remote(src, dst, s, r, **where)
        cp.start()
        sent.append(cp)
        flow[name] = cp

    def cols(k):
        return pl.ds(chunks[k][0], chunks[k][1])

    def piece(k, of, half):
        return part.at[rows(of * 2 * n + half * n, n), cols(k)]

    def at(ref, k):
        return ref.at[:, cols(k)]

    def rs_far(k):
        send((k, 0), piece(k, far, 0), at(via_l, k), rs_s.at[k, 0], rs_r.at[k, 0], dp_1=right)
        send((k, 1), piece(k, far, 1), at(via_r, k), rs_s.at[k, 1], rs_r.at[k, 1], dp_1=left)

    def rs_near(k):
        send((k, 2), piece(k, right, 1), at(raw_l, k), rs_s.at[k, 2], rs_r.at[k, 2], dp_1=right)
        send((k, 3), piece(k, left, 0), at(raw_r, k), rs_s.at[k, 3], rs_r.at[k, 3], dp_1=left)

    def load(ref, k, where=slice(None)):
        return ref[where, cols(k)].astype(f32)

    def rs_turn(k):
        flow[k, 0].wait_recv()
        turn_r[:, cols(k)] = (load(via_l, k) + load(part, k, rows(right * 2 * n, n))).astype(turn_r.dtype)
        send((k, 4), at(turn_r, k), at(add_l, k), rs_s.at[k, 4], rs_r.at[k, 4], dp_1=right)
        flow[k, 1].wait_recv()
        turn_l[:, cols(k)] = (load(via_r, k) + load(part, k, rows(left * 2 * n + n, n, n))).astype(turn_l.dtype)
        send((k, 5), at(turn_l, k), at(add_r, k), rs_s.at[k, 5], rs_r.at[k, 5], dp_1=left)

    def total(k, half):
        if half == 0:
            return load(part, k, rows(x * 2 * n, n)) + load(add_l, k) + load(raw_r, k)
        return load(part, k, rows(x * 2 * n + n, n, n)) + load(add_r, k) + load(raw_l, k)

    def rs_sum(k):
        for i in (2, 3, 4, 5):
            flow[k, i].wait_recv()
        for mine in range(2):

            @pl.when(zl == mine)
            def _():
                zsend[:, cols(k)] = total(k, 1 - mine).astype(zsend.dtype)

        send((k, 6), at(zsend, k), at(zrecv, k), rs_s.at[k, 6], rs_r.at[k, 6], dp_2=1 - zl)
        for mine in range(2):

            @pl.when(zl == mine)
            def _():
                new_first[:, cols(k)] = total(k, mine)

    def adam(k):
        flow[k, 6].wait_recv()
        grad = new_first[:, cols(k)] + load(zrecv, k)
        m1 = 0.9 * first_m[:, cols(k)] + 0.1 * grad
        m2 = 0.999 * second_m[:, cols(k)] + 0.001 * grad * grad
        new_first[:, cols(k)] = m1
        new_second[:, cols(k)] = m2
        first_fix = 1.0 - 0.9**STEP
        second_fix = 1.0 - 0.999**STEP
        both[rows(zl * n, n), cols(k)] = (
            m1 / first_fix / (jnp.sqrt(m2 / second_fix) + 1e-08)
        ).astype(both.dtype)
        own = both.at[rows(zl * n, n), cols(k)]
        send((k, "d"), own, own, d_s.at[k], d_r.at[k], dp_2=1 - zl)

    def line(k):
        if chunks[k][2] == 0:
            return "dp_1", "dp_0", x, y, 1, 4
        return "dp_0", "dp_1", y, x, 4, 1

    def region(k, p1, p2, start, size):
        f1, f2 = line(k)[4:]
        return full.at[rows((p1 * f1 + p2 * f2) * 2 * n + start, size, n), cols(k)]

    def pass_on(k, i, axis, to, where, src=None):
        send((k, "a", i), where if src is None else src, where, ag_s.at[k, i], ag_r.at[k, i], **{axis: to})

    def ag_own(k):
        first, second, at1, at2 = line(k)[:4]
        landed(both.at[rows((1 - zl) * n, n), cols(k)], d_r.at[k])
        src, here = both.at[:, cols(k)], region(k, at1, at2, 0, 2 * n)
        pass_on(k, 0, first, plus(at1, 1), here, src)
        pass_on(k, 1, first, plus(at1, 3), here, src)
        pass_on(k, 4, second, plus(at2, 1), here, src)
        pass_on(k, 8, second, plus(at2, 3), here, src)
        pltpu.make_async_copy(src, here, put_sem.at[k]).start()

    def ag_first(k):
        first, second, at1, at2 = line(k)[:4]
        for j, d, to, half in ((0, 3, 1, 0), (1, 1, 3, 1)):
            landed(region(k, plus(at1, d), at2, 0, 2 * n), ag_r.at[k, j])
            pass_on(k, 2 + j, first, plus(at1, to), region(k, plus(at1, d), at2, half * n, n))
            here = region(k, plus(at1, d), at2, 0, 2 * n)
            pass_on(k, 5 + j, second, plus(at2, 1), here)
            pass_on(k, 9 + j, second, plus(at2, 3), here)

    def ag_far(k):
        first, second, at1, at2 = line(k)[:4]
        landed(region(k, plus(at1, 2), at2, 0, n), ag_r.at[k, 2])
        landed(region(k, plus(at1, 2), at2, n, n), ag_r.at[k, 3])
        here = region(k, plus(at1, 2), at2, 0, 2 * n)
        pass_on(k, 7, second, plus(at2, 1), here)
        pass_on(k, 11, second, plus(at2, 3), here)

    def ag_second(k, i):
        first, second, at1, at2 = line(k)[:4]
        d = (0, 3, 1, 2)[i]
        landed(region(k, plus(at1, d), plus(at2, 3), 0, 2 * n), ag_r.at[k, 4 + i])
        pass_on(k, 12 + i, second, plus(at2, 1), region(k, plus(at1, d), plus(at2, 3), 0, n))
        landed(region(k, plus(at1, d), plus(at2, 1), 0, 2 * n), ag_r.at[k, 8 + i])
        pass_on(k, 16 + i, second, plus(at2, 3), region(k, plus(at1, d), plus(at2, 1), n, n))

    def ag_last(k):
        first, second, at1, at2 = line(k)[:4]
        for i, d in enumerate((0, 3, 1, 2)):
            landed(region(k, plus(at1, d), plus(at2, 2), 0, n), ag_r.at[k, 12 + i])
            landed(region(k, plus(at1, d), plus(at2, 2), n, n), ag_r.at[k, 16 + i])
        landed(region(k, at1, at2, 0, 2 * n), put_sem.at[k])

    def own_rows():
        take.wait()
        keep.start()
        for i, who in enumerate(others):
            send(("p", i), stage, here, p_s.at[i], p_r.at[i], **who)

    take = pltpu.make_async_copy(proj, stage, loc_sem.at[0])
    take.start()
    here = prow.at[:, rows((h * 2 + c) * lanes, lanes)]
    keep = pltpu.make_async_copy(stage, here, loc_sem.at[1])

    rs_far(0)
    rs_near(0)
    rs_far(1)
    rs_turn(0)
    rs_near(1)
    rs_far(2)
    rs_sum(0)
    rs_turn(1)
    rs_near(2)
    adam(0)
    rs_sum(1)
    rs_turn(2)
    ag_own(0)
    adam(1)
    rs_sum(2)
    ag_own(1)
    adam(2)
    ag_first(0)
    ag_own(2)
    own_rows()
    ag_first(1)
    ag_far(0)
    ag_first(2)
    ag_far(1)
    ag_far(2)
    for i in range(4):
        for k in range(3):
            ag_second(k, i)
    for k in range(3):
        ag_last(k)
    for i, who in enumerate(others):
        frm = plus(h, 4 - (i + 1) // 2) * 2 + lax.rem(c + (i + 1) % 2, 2)
        landed(prow.at[:, rows(frm * lanes, lanes)], p_r.at[i])
    keep.wait()
    for cp in sent:
        cp.wait_send()


def update(part, first_moment, second_moment, projector):
    n, cols = first_moment.shape
    feat, lanes = projector.shape
    bf, f32 = jnp.bfloat16, jnp.float32
    third = cols // 384 * 128
    chunks = ((0, third, 0), (third, third, 0), (2 * third, cols - 2 * third, 1))
    slot = pltpu.VMEM((n, cols), bf)
    count = len(chunks)
    return pl.pallas_call(
        functools.partial(update_kernel, chunks),
        name="update",
        out_shape=(
            jax.ShapeDtypeStruct((n, cols), f32),
            jax.ShapeDtypeStruct((n, cols), f32),
            jax.ShapeDtypeStruct((32 * n, cols), bf),
            jax.ShapeDtypeStruct((feat, 8 * lanes), bf),
        ),
        in_specs=[VMEM, VMEM, VMEM, ANY],
        out_specs=(VMEM, VMEM, ANY, ANY),
        scratch_shapes=[slot] * 10 + [
            pltpu.VMEM((2 * n, cols), bf),
            pltpu.VMEM((feat, lanes), bf),
            DMA((2,)),
            DMA((count,)),
            DMA((count, 7)), DMA((count, 7)),
            DMA((count,)), DMA((count,)),
            DMA((count, 20)), DMA((count, 20)),
            DMA((7,)), DMA((7,)),
        ],
        compiler_params=pltpu.CompilerParams(
            collective_id=1, has_side_effects=True, vmem_limit_bytes=12 << 20
        ),
    )(part, first_moment, second_moment, projector)


def per_device(inputs, projector, out_grads, weights, first_moment, second_moment):
    projected, grads = gather_projected(inputs, projector, out_grads)
    part = lax.dot_general(
        projected, grads, (((0,), (0,)), ((), ())), preferred_element_type=jnp.float32
    ).astype(jnp.bfloat16)
    new_first, new_second, full, ranks = update(part, first_moment, second_moment, projector)
    lifted = jnp.dot(ranks, full, preferred_element_type=jnp.float32)
    new_weights = (weights.astype(jnp.float32) - 2.0 * lifted).astype(jnp.bfloat16)
    return (new_weights, new_first, new_second)


def solution(mesh):
    finer = Mesh(mesh.devices.reshape(4, 4, 2, 4, 2), AXES)
    spec = P(DP, MP)
    return jax.shard_map(
        per_device, mesh=finer, in_specs=(spec,) * 6, out_specs=(spec,) * 3, check_vma=False
    )
```

```python
import functools

import jax
import jax.numpy as jnp
from jax import lax
from jax.experimental import pallas as pl
from jax.experimental.pallas import tpu as pltpu
from jax.sharding import Mesh
from jax.sharding import PartitionSpec as P

STEP = 1000
AXES = ("dp_0", "dp_1", "dp_2", "mp_0", "mp_1")
DP = AXES[:3]
MP = AXES[3:]
MESH = pl.DeviceIdType.MESH
ANY = pl.BlockSpec(memory_space=pl.ANY)
VMEM = pl.BlockSpec(memory_space=pltpu.VMEM)
DMA = pltpu.SemaphoreType.DMA


def in_hbm(x):
    return pltpu.with_memory_space_constraint(x, pltpu.HBM)


def place():
    return tuple(lax.axis_index(a) for a in AXES)


def remote(src, dst, send_sem, recv_sem, **where):
    return pltpu.make_async_remote_copy(
        src_ref=src,
        dst_ref=dst,
        send_sem=send_sem,
        recv_sem=recv_sem,
        device_id=where,
        device_id_type=MESH,
    )


def landed(dst, sem):
    pltpu.make_async_copy(dst, dst, sem).wait()


def rows(start, size, unit=None):
    return pl.ds(pl.multiple_of(start, unit or size), size)


def greet(peers, extra=None):
    barrier = pltpu.get_barrier_semaphore()
    for peer in peers:
        pl.semaphore_signal(barrier, inc=1, device_id=peer, device_id_type=MESH)
    count = len(peers)
    if extra is not None:
        peer, present = extra

        @pl.when(present)
        def _():
            pl.semaphore_signal(barrier, inc=1, device_id=peer, device_id_type=MESH)

        count = count + present.astype(jnp.int32)
    pl.semaphore_wait(barrier, count)


def projected_kernel(
    inp, proj, grads, pa, ga,
    inp4, pq, own, out_half, half_in, via_d, via_u, raw_d, raw_u, turn_u, turn_d, add_d, add_u, g_own,
    loc_sem, in_s, in_r, g_s, g_r, sw_s, pq_r, ring_s, ring_r, half_s, half_r, rs_s, rs_r, sh_s, sh_r,
):
    y, x, zl, h, c = place()
    up, down = lax.rem(y + 1, 4), lax.rem(y + 3, 4)
    right, left = lax.rem(x + 1, 4), lax.rem(x + 3, 4)
    above, below = lax.rem(h + 1, 4), lax.rem(h + 3, 4)
    tok = inp.shape[0]
    half = tok // 2
    feat, lanes = proj.shape
    wide = ga.shape[1]
    peers = [
        {"dp_0": up}, {"dp_0": down}, {"dp_1": right}, {"dp_1": left},
        {"mp_0": above}, {"mp_0": below}, {"mp_1": 1 - c},
        {"dp_2": 1 - zl},
        {"dp_0": h, "mp_0": y, "mp_1": 1 - c},
    ]
    greet(peers, ({"dp_0": h, "mp_0": y}, y != h))

    sent = []

    def send(src, dst, s, r, **where):
        cp = remote(src, dst, s, r, **where)
        cp.start()
        sent.append(cp)
        return cp

    core = x // 2

    def block(i, z, k):
        return pq.at[rows((i * 2 + z) * feat, feat), pl.ds(k * lanes, lanes)]

    def part_of(i, z, k, p):
        return pq.at[rows((i * 2 + z) * feat + p * (feat // 2), feat // 2), pl.ds(k * lanes, lanes)]

    spot = pq.at[rows((lax.rem(x, 2) * 2 + zl) * feat, feat), rows(c * lanes, lanes)]
    mark = (lax.rem(x, 2) * 2 + zl) * 2 + c
    at_home = (y == h) & (c == core)
    swap = remote(proj, spot, sw_s.at[0], pq_r.at[mark], dp_0=h, mp_0=y, mp_1=core)
    stay = pltpu.make_async_copy(proj, spot, pq_r.at[mark])

    @pl.when(jnp.logical_not(at_home))
    def _():
        swap.start()

    @pl.when(at_home)
    def _():
        stay.start()

    def slot(k, start, size):
        return inp4.at[k // 2, pl.ds((k % 2) * tok + start, size)]

    lo, hi = pl.ds(0, half), pl.ds(half, half)
    in_up = send(inp.at[lo], slot(1, 0, half), in_s.at[0], in_r.at[0], dp_0=up)
    in_dn = send(inp.at[hi], slot(3, half, half), in_s.at[1], in_r.at[1], dp_0=down)
    in_up2 = send(inp.at[hi], slot(1, half, half), in_s.at[2], in_r.at[2], dp_0=up)
    in_dn2 = send(inp.at[lo], slot(3, 0, half), in_s.at[3], in_r.at[3], dp_0=down)
    own_in = pltpu.make_async_copy(inp, slot(0, 0, tok), loc_sem.at[0])
    own_in.start()
    own_g = pltpu.make_async_copy(grads.at[:, pl.ds(0, wide)], g_own, loc_sem.at[1])
    own_g.start()

    def away(i):
        return lax.rem(x + 4 - (2 * c + i), 4)

    later = []

    def ring(k, dz, stage):
        z = lax.rem(zl + dz, 2)
        for i in range(2):
            m = (i * 2 + z) * 2 + k
            whole = block(i, z, k)
            if stage == 0:
                fr = remote(whole, whole, ring_s.at[m, 0], pq_r.at[m], dp_1=right)
                fl = remote(whole, whole, ring_s.at[m, 1], pq_r.at[m], dp_1=left)
                both = (fr, fl)
                if dz == 0:
                    both = (remote(whole, whole, ring_s.at[m, 2], pq_r.at[m], dp_2=1 - zl), fr, fl)

                @pl.when(away(i) == 0)
                def _():
                    landed(whole, pq_r.at[m])
                    for cp in both:
                        cp.start()

                later.append((away(i) == 0, both))
            if stage == 1:
                for d, p, to in ((1, 0, right), (3, 1, left)):
                    some = part_of(i, z, k, p)
                    fw = remote(some, some, ring_s.at[m, p], ring_r.at[m, p], dp_1=to)

                    @pl.when(away(i) == d)
                    def _():
                        landed(whole, pq_r.at[m])
                        fw.start()

                    later.append((away(i) == d, (fw,)))
            if stage == 2:

                @pl.when(away(i) == 2)
                def _():
                    landed(part_of(i, z, k, 0), ring_r.at[m, 0])
                    landed(part_of(i, z, k, 1), ring_r.at[m, 1])

    ring(0, 0, 0)
    ring(1, 0, 0)
    in_up.wait_recv()
    fw_up = send(slot(1, 0, half), slot(2, 0, half), in_s.at[4], in_r.at[4], dp_0=up)
    in_dn.wait_recv()
    fw_dn = send(slot(3, half, half), slot(2, half, half), in_s.at[5], in_r.at[5], dp_0=down)
    ring(0, 1, 0)
    ring(1, 1, 0)

    def g_from(start, size):
        return ga.at[pl.ds(start, size)]

    g_up = send(grads.at[lo, pl.ds(0, wide)], g_from(tok, half), g_s.at[0], g_r.at[0], dp_0=up)
    g_dn = send(grads.at[hi, pl.ds(0, wide)], g_from(3 * tok + half, half), g_s.at[1], g_r.at[1], dp_0=down)
    g_up2 = send(grads.at[hi, pl.ds(0, wide)], g_from(tok + half, half), g_s.at[2], g_r.at[2], dp_0=up)
    g_dn2 = send(grads.at[lo, pl.ds(0, wide)], g_from(3 * tok, half), g_s.at[3], g_r.at[3], dp_0=down)
    own_g.wait()
    put_g = pltpu.make_async_copy(g_own, g_from(0, tok), loc_sem.at[2])
    put_g.start()
    for k in range(2):
        for dz in range(2):
            ring(k, dz, 1)
    own_in.wait()
    in_up2.wait_recv()
    in_dn2.wait_recv()
    fw_up.wait_recv()
    fw_dn.wait_recv()

    pairs = []
    for k in range(2):
        for dz in range(2):
            ring(k, dz, 2)
        here = pl.ds(k * lanes, lanes)
        for t in range(2):
            out_half[k, pl.ds(t * tok, tok)] = jnp.dot(
                inp4[1 - c, pl.ds(t * tok, tok)], pq[:, here], preferred_element_type=jnp.float32
            )
        pairs.append(send(out_half.at[k], half_in.at[k], half_s.at[k], half_r.at[k], mp_1=1 - c))
        for t in range(2):
            own[k, pl.ds(t * tok, tok)] = jnp.dot(
                inp4[c, pl.ds(t * tok, tok)], pq[:, here], preferred_element_type=jnp.float32
            )

    cut = 2 * tok // 4
    q = cut // 2
    beyond = lax.rem(h + 2, 4)
    flow = {}

    def piece(k, of, p):
        return own.at[k, rows(of * cut + p * q, q)]

    def value(k, of, p):
        return own[k, rows(of * cut + p * q, q)]

    for k in range(2):
        pairs[k].wait_recv()
        own[k] += half_in[k]
        flow[k, 0] = send(piece(k, beyond, 0), via_d.at[k], rs_s.at[k, 0], rs_r.at[k, 0], mp_0=above)
        flow[k, 1] = send(piece(k, beyond, 1), via_u.at[k], rs_s.at[k, 1], rs_r.at[k, 1], mp_0=below)
        flow[k, 2] = send(piece(k, above, 1), raw_d.at[k], rs_s.at[k, 2], rs_r.at[k, 2], mp_0=above)
        flow[k, 3] = send(piece(k, below, 0), raw_u.at[k], rs_s.at[k, 3], rs_r.at[k, 3], mp_0=below)
    for k in range(2):
        flow[k, 0].wait_recv()
        turn_u[k] = via_d[k] + value(k, above, 0)
        flow[k, 4] = send(turn_u.at[k], add_d.at[k], rs_s.at[k, 4], rs_r.at[k, 4], mp_0=above)
        flow[k, 1].wait_recv()
        turn_d[k] = via_u[k] + value(k, below, 1)
        flow[k, 5] = send(turn_d.at[k], add_u.at[k], rs_s.at[k, 5], rs_r.at[k, 5], mp_0=below)

    def share(k, of, start=0, size=cut, who=c):
        return pa.at[rows(who * 2 * tok + of * cut + start, size, size), pl.ds(k * lanes, lanes)]

    for k in range(2):
        for i in (2, 3, 4, 5):
            flow[k, i].wait_recv()
        top = value(k, h, 0) + add_d[k] + raw_u[k]
        low = value(k, h, 1) + add_u[k] + raw_d[k]
        pa[rows(c * 2 * tok + h * cut, cut), pl.ds(k * lanes, lanes)] = jnp.concatenate(
            [top, low], axis=0
        ).astype(pa.dtype)
        flow[k, 6] = send(share(k, h), share(k, h), sh_s.at[k, 0], sh_r.at[k, 0], mp_0=above)
        flow[k, 7] = send(share(k, h), share(k, h), sh_s.at[k, 1], sh_r.at[k, 1], mp_0=below)
        send(share(k, h), share(k, h), sh_s.at[k, 4], sh_r.at[k, 4], mp_1=1 - c)
    g_up.wait_recv()
    gf_up = send(g_from(tok, half), g_from(2 * tok, half), g_s.at[4], g_r.at[4], dp_0=up)
    g_dn.wait_recv()
    gf_dn = send(
        g_from(3 * tok + half, half), g_from(2 * tok + half, half), g_s.at[5], g_r.at[5], dp_0=down
    )
    for k in range(2):
        landed(share(k, below), sh_r.at[k, 0])
        send(share(k, below, 0, q), share(k, below, 0, q), sh_s.at[k, 2], sh_r.at[k, 2], mp_0=above)
        send(share(k, below), share(k, below), sh_s.at[k, 5], sh_r.at[k, 5], mp_1=1 - c)
        landed(share(k, above), sh_r.at[k, 1])
        send(share(k, above, q, q), share(k, above, q, q), sh_s.at[k, 3], sh_r.at[k, 3], mp_0=below)
        send(share(k, above), share(k, above), sh_s.at[k, 6], sh_r.at[k, 6], mp_1=1 - c)
    for k in range(2):
        landed(share(k, beyond, 0, q), sh_r.at[k, 2])
        landed(share(k, beyond, q, q), sh_r.at[k, 3])
        send(share(k, beyond), share(k, beyond), sh_s.at[k, 7], sh_r.at[k, 7], mp_1=1 - c)
    for k in range(2):
        for i, of in enumerate((h, below, above, beyond)):
            landed(share(k, of, who=1 - c), sh_r.at[k, 4 + i])
    g_up2.wait_recv()
    g_dn2.wait_recv()
    gf_up.wait_recv()
    gf_dn.wait_recv()
    put_g.wait()
    for cp in sent:
        cp.wait_send()
    for when, copies in later + [(jnp.logical_not(at_home), (swap,))]:

        @pl.when(when)
        def _():
            for cp in copies:
                cp.wait_send()


def gather_projected(inputs, projector, out_grads):
    tok, feats = inputs.shape
    feat, lanes = projector.shape
    wide = out_grads.shape[1]
    bf, f32 = jnp.bfloat16, jnp.float32
    small = pltpu.VMEM((2, tok // 4, lanes), f32)
    return pl.pallas_call(
        projected_kernel,
        name="gather_projected",
        out_shape=(
            jax.ShapeDtypeStruct((4 * tok, 2 * lanes), bf),
            jax.ShapeDtypeStruct((4 * tok, wide), bf),
        ),
        in_specs=[ANY] * 3,
        out_specs=(VMEM, ANY),
        scratch_shapes=[
            pltpu.VMEM((2, 2 * tok, feats), bf),
            pltpu.VMEM((4 * feat, 2 * lanes), bf),
            pltpu.VMEM((2, 2 * tok, lanes), f32),
            pltpu.VMEM((2, 2 * tok, lanes), f32),
            pltpu.VMEM((2, 2 * tok, lanes), f32),
            *[small] * 8,
            pltpu.VMEM((tok, wide), bf),
            DMA((3,)),
            DMA((6,)), DMA((6,)),
            DMA((6,)), DMA((6,)),
            DMA((1,)), DMA((8,)),
            DMA((8, 3)), DMA((8, 2)),
            DMA((2,)), DMA((2,)),
            DMA((2, 6)), DMA((2, 6)),
            DMA((2, 8)), DMA((2, 8)),
        ],
        compiler_params=pltpu.CompilerParams(
            collective_id=0, has_side_effects=True, vmem_limit_bytes=12 << 20
        ),
    )(in_hbm(inputs), in_hbm(projector), in_hbm(out_grads))


def update_kernel(
    chunks, part, first_in, second_in, proj, new_first, new_second, full, prow,
    raw_l, raw_r, via_l, via_r, turn_r, turn_l, add_l, add_r, zsend, zrecv, both, stage, first_m, second_m,
    loc_sem, put_sem, rs_s, rs_r, d_s, d_r, ag_s, ag_r, p_s, p_r,
):
    y, x, zl, h, c = place()
    n = first_in.shape[0]
    lanes = proj.shape[1]
    f32 = jnp.float32
    right, left, far = lax.rem(x + 1, 4), lax.rem(x + 3, 4), lax.rem(x + 2, 4)

    def plus(at, d):
        return lax.rem(at + d, 4)

    others = []
    for dh in range(4):
        for dc in range(2):
            if dh:
                others.append({"mp_0": plus(h, dh), "mp_1": lax.rem(c + dc, 2)})
            elif dc:
                others.append({"mp_1": 1 - c})
    peers = [{"dp_2": 1 - zl}]
    for axis, at in (("dp_0", y), ("dp_1", x)):
        peers += [{axis: plus(at, 1)}, {axis: plus(at, 3)}]
    greet(peers + others)

    sent = []
    flow = {}

    def send(name, src, dst, s, r, **where):
        cp = remote(src, dst, s, r, **where)
        cp.start()
        sent.append(cp)
        flow[name] = cp

    def cols(k):
        return pl.ds(chunks[k][0], chunks[k][1])

    def piece(k, of, half):
        return part.at[rows(of * 2 * n + half * n, n), cols(k)]

    def mine_of(k, start):
        return part[rows(start, n), cols(k)].astype(f32)

    def at(ref, k):
        return ref.at[:, cols(k)]

    def rs_far(k):
        send((k, 0), piece(k, far, 0), at(via_l, k), rs_s.at[k, 0], rs_r.at[k, 0], dp_1=right)
        send((k, 1), piece(k, far, 1), at(via_r, k), rs_s.at[k, 1], rs_r.at[k, 1], dp_1=left)

    def rs_near(k):
        send((k, 2), piece(k, right, 1), at(raw_l, k), rs_s.at[k, 2], rs_r.at[k, 2], dp_1=right)
        send((k, 3), piece(k, left, 0), at(raw_r, k), rs_s.at[k, 3], rs_r.at[k, 3], dp_1=left)

    def load(ref, k, where=slice(None)):
        return ref[where, cols(k)].astype(f32)

    def rs_turn(k):
        flow[k, 0].wait_recv()
        turn_r[:, cols(k)] = (load(via_l, k) + mine_of(k, right * 2 * n)).astype(turn_r.dtype)
        send((k, 4), at(turn_r, k), at(add_l, k), rs_s.at[k, 4], rs_r.at[k, 4], dp_1=right)
        flow[k, 1].wait_recv()
        turn_l[:, cols(k)] = (load(via_r, k) + mine_of(k, left * 2 * n + n)).astype(turn_l.dtype)
        send((k, 5), at(turn_l, k), at(add_r, k), rs_s.at[k, 5], rs_r.at[k, 5], dp_1=left)

    def total(k, half):
        if half == 0:
            return mine_of(k, x * 2 * n) + load(add_l, k) + load(raw_r, k)
        return mine_of(k, x * 2 * n + n) + load(add_r, k) + load(raw_l, k)

    def rs_sum(k):
        for i in (2, 3, 4, 5):
            flow[k, i].wait_recv()
        for mine in range(2):

            @pl.when(zl == mine)
            def _():
                zsend[:, cols(k)] = total(k, 1 - mine).astype(zsend.dtype)

        send((k, 6), at(zsend, k), at(zrecv, k), rs_s.at[k, 6], rs_r.at[k, 6], dp_2=1 - zl)
        for mine in range(2):

            @pl.when(zl == mine)
            def _():
                new_first[:, cols(k)] = total(k, mine)

    def adam(k):
        flow[k, 6].wait_recv()
        grad = new_first[:, cols(k)] + load(zrecv, k)
        m1 = 0.9 * first_m[:, cols(k)] + 0.1 * grad
        m2 = 0.999 * second_m[:, cols(k)] + 0.001 * grad * grad
        new_first[:, cols(k)] = m1
        new_second[:, cols(k)] = m2
        first_fix = 1.0 - 0.9**STEP
        second_fix = 1.0 - 0.999**STEP
        both[rows(zl * n, n), cols(k)] = (
            m1 / first_fix / (jnp.sqrt(m2 / second_fix) + 1e-08)
        ).astype(both.dtype)
        own = both.at[rows(zl * n, n), cols(k)]
        send((k, "d"), own, own, d_s.at[k], d_r.at[k], dp_2=1 - zl)

    def line(k):
        if chunks[k][2] == 0:
            return "dp_1", "dp_0", x, y, 1, 4
        return "dp_0", "dp_1", y, x, 4, 1

    def region(k, p1, p2, start, size):
        f1, f2 = line(k)[4:]
        return full.at[rows((p1 * f1 + p2 * f2) * 2 * n + start, size, n), cols(k)]

    def pass_on(k, i, axis, to, where, src=None):
        send((k, "a", i), where if src is None else src, where, ag_s.at[k, i], ag_r.at[k, i], **{axis: to})

    def ag_own(k):
        first, second, at1, at2 = line(k)[:4]
        landed(both.at[rows((1 - zl) * n, n), cols(k)], d_r.at[k])
        src, here = both.at[:, cols(k)], region(k, at1, at2, 0, 2 * n)
        pass_on(k, 0, first, plus(at1, 1), here, src)
        pass_on(k, 1, first, plus(at1, 3), here, src)
        pass_on(k, 4, second, plus(at2, 1), here, src)
        pass_on(k, 8, second, plus(at2, 3), here, src)
        pltpu.make_async_copy(src, here, put_sem.at[k]).start()

    def ag_first(k):
        first, second, at1, at2 = line(k)[:4]
        for j, d, to, half in ((0, 3, 1, 0), (1, 1, 3, 1)):
            landed(region(k, plus(at1, d), at2, 0, 2 * n), ag_r.at[k, j])
            pass_on(k, 2 + j, first, plus(at1, to), region(k, plus(at1, d), at2, half * n, n))
            here = region(k, plus(at1, d), at2, 0, 2 * n)
            pass_on(k, 5 + j, second, plus(at2, 1), here)
            pass_on(k, 9 + j, second, plus(at2, 3), here)

    def ag_far(k):
        first, second, at1, at2 = line(k)[:4]
        landed(region(k, plus(at1, 2), at2, 0, n), ag_r.at[k, 2])
        landed(region(k, plus(at1, 2), at2, n, n), ag_r.at[k, 3])
        here = region(k, plus(at1, 2), at2, 0, 2 * n)
        pass_on(k, 7, second, plus(at2, 1), here)
        pass_on(k, 11, second, plus(at2, 3), here)

    def ag_second(k, i):
        first, second, at1, at2 = line(k)[:4]
        d = (0, 3, 1, 2)[i]
        landed(region(k, plus(at1, d), plus(at2, 3), 0, 2 * n), ag_r.at[k, 4 + i])
        pass_on(k, 12 + i, second, plus(at2, 1), region(k, plus(at1, d), plus(at2, 3), 0, n))
        landed(region(k, plus(at1, d), plus(at2, 1), 0, 2 * n), ag_r.at[k, 8 + i])
        pass_on(k, 16 + i, second, plus(at2, 3), region(k, plus(at1, d), plus(at2, 1), n, n))

    def ag_last(k):
        first, second, at1, at2 = line(k)[:4]
        for i, d in enumerate((0, 3, 1, 2)):
            landed(region(k, plus(at1, d), plus(at2, 2), 0, n), ag_r.at[k, 12 + i])
            landed(region(k, plus(at1, d), plus(at2, 2), n, n), ag_r.at[k, 16 + i])
        landed(region(k, at1, at2, 0, 2 * n), put_sem.at[k])

    def own_rows():
        take.wait()
        keep.start()
        for i, who in enumerate(others):
            send(("p", i), stage, here, p_s.at[i], p_r.at[i], **who)

    state = [
        pltpu.make_async_copy(first_in, first_m, loc_sem.at[2]),
        pltpu.make_async_copy(second_in, second_m, loc_sem.at[3]),
    ]
    for cp in state:
        cp.start()
    take = pltpu.make_async_copy(proj, stage, loc_sem.at[0])
    take.start()
    here = prow.at[:, rows((h * 2 + c) * lanes, lanes)]
    keep = pltpu.make_async_copy(stage, here, loc_sem.at[1])

    rs_far(0)
    rs_near(0)
    rs_far(1)
    rs_turn(0)
    rs_near(1)
    rs_far(2)
    rs_sum(0)
    rs_turn(1)
    rs_near(2)
    for cp in state:
        cp.wait()
    adam(0)
    rs_sum(1)
    rs_turn(2)
    ag_own(0)
    adam(1)
    rs_sum(2)
    ag_own(1)
    adam(2)
    ag_first(0)
    ag_own(2)
    own_rows()
    ag_first(1)
    ag_far(0)
    ag_first(2)
    ag_far(1)
    ag_far(2)
    for i in range(4):
        for k in range(3):
            ag_second(k, i)
    for k in range(3):
        ag_last(k)
    for i, who in enumerate(others):
        frm = plus(h, 4 - (i + 1) // 2) * 2 + lax.rem(c + (i + 1) % 2, 2)
        landed(prow.at[:, rows(frm * lanes, lanes)], p_r.at[i])
    keep.wait()
    for cp in sent:
        cp.wait_send()


def split(cols):
    third = cols // 384 * 128
    return ((0, third, 0), (third, third, 0), (2 * third, cols - 2 * third, 1))


def update(part, first_moment, second_moment, projector):
    n, cols = first_moment.shape
    feat, lanes = projector.shape
    bf, f32 = jnp.bfloat16, jnp.float32
    chunks = split(cols)
    slot = pltpu.VMEM((n, cols), bf)
    count = len(chunks)
    return pl.pallas_call(
        functools.partial(update_kernel, chunks),
        name="update",
        out_shape=(
            jax.ShapeDtypeStruct((n, cols), f32),
            jax.ShapeDtypeStruct((n, cols), f32),
            jax.ShapeDtypeStruct((32 * n, cols), bf),
            jax.ShapeDtypeStruct((feat, 8 * lanes), bf),
        ),
        in_specs=[VMEM, ANY, ANY, ANY],
        out_specs=(VMEM, VMEM, ANY, ANY),
        scratch_shapes=[slot] * 10 + [
            pltpu.VMEM((2 * n, cols), bf),
            pltpu.VMEM((feat, lanes), bf),
            pltpu.VMEM((n, cols), f32),
            pltpu.VMEM((n, cols), f32),
            DMA((4,)),
            DMA((count,)),
            DMA((count, 7)), DMA((count, 7)),
            DMA((count,)), DMA((count,)),
            DMA((count, 20)), DMA((count, 20)),
            DMA((7,)), DMA((7,)),
        ],
        compiler_params=pltpu.CompilerParams(
            collective_id=1, has_side_effects=True, vmem_limit_bytes=16 << 20
        ),
    )(part, *(in_hbm(v) for v in (first_moment, second_moment, projector)))


def per_device(inputs, projector, out_grads, weights, first_moment, second_moment):
    projected, grads = gather_projected(inputs, projector, out_grads)
    part = lax.dot_general(
        projected, grads, (((0,), (0,)), ((), ())), preferred_element_type=jnp.float32
    ).astype(jnp.bfloat16)
    new_first, new_second, full, ranks = update(part, first_moment, second_moment, projector)
    lifted = jnp.dot(ranks, full, preferred_element_type=jnp.float32)
    new_weights = (weights.astype(jnp.float32) - 2.0 * lifted).astype(jnp.bfloat16)
    return (new_weights, new_first, new_second)


def solution(mesh):
    finer = Mesh(mesh.devices.reshape(4, 4, 2, 4, 2), AXES)
    spec = P(DP, MP)
    return jax.shard_map(
        per_device, mesh=finer, in_specs=(spec,) * 6, out_specs=(spec,) * 3, check_vma=False
    )
```

```python
import functools

import jax
import jax.numpy as jnp
from jax import lax
from jax.experimental import pallas as pl
from jax.experimental.pallas import tpu as pltpu
from jax.sharding import Mesh
from jax.sharding import PartitionSpec as P

STEP = 1000
AXES = ("dp_0", "dp_1", "dp_2", "mp_0", "mp_1")
DP = AXES[:3]
MP = AXES[3:]
MESH = pl.DeviceIdType.MESH
ANY = pl.BlockSpec(memory_space=pl.ANY)
VMEM = pl.BlockSpec(memory_space=pltpu.VMEM)
DMA = pltpu.SemaphoreType.DMA


def in_hbm(x):
    return pltpu.with_memory_space_constraint(x, pltpu.HBM)


def place():
    return tuple(lax.axis_index(a) for a in AXES)


def remote(src, dst, send_sem, recv_sem, **where):
    return pltpu.make_async_remote_copy(
        src_ref=src,
        dst_ref=dst,
        send_sem=send_sem,
        recv_sem=recv_sem,
        device_id=where,
        device_id_type=MESH,
    )


def landed(dst, sem):
    pltpu.make_async_copy(dst, dst, sem).wait()


def rows(start, size, unit=None):
    return pl.ds(pl.multiple_of(start, unit or size), size)


def greet(peers, extra=None):
    barrier = pltpu.get_barrier_semaphore()
    for peer in peers:
        pl.semaphore_signal(barrier, inc=1, device_id=peer, device_id_type=MESH)
    count = len(peers)
    if extra is not None:
        peer, present = extra

        @pl.when(present)
        def _():
            pl.semaphore_signal(barrier, inc=1, device_id=peer, device_id_type=MESH)

        count = count + present.astype(jnp.int32)
    pl.semaphore_wait(barrier, count)


def projected_body(
    inp, proj, grads, pa, ga,
    inp4, pq, own, out_half, half_in, via_d, via_u, raw_d, raw_u, turn_u, turn_d, add_d, add_u,
    loc_sem, in_s, in_r, g_s, g_r, sw_s, pq_r, ring_s, ring_r, half_s, half_r, rs_s, rs_r, sh_s, sh_r,
):
    y, x, zl, h, c = place()
    up, down = lax.rem(y + 1, 4), lax.rem(y + 3, 4)
    right, left = lax.rem(x + 1, 4), lax.rem(x + 3, 4)
    above, below = lax.rem(h + 1, 4), lax.rem(h + 3, 4)
    tok = inp.shape[0]
    half = tok // 2
    feat, lanes = proj.shape
    wide = ga.shape[1]
    sent = []

    def send(src, dst, s, r, **where):
        cp = remote(src, dst, s, r, **where)
        cp.start()
        sent.append(cp)
        return cp

    core = x // 2

    def block(i, z, k):
        return pq.at[rows((i * 2 + z) * feat, feat), pl.ds(k * lanes, lanes)]

    def part_of(i, z, k, p):
        return pq.at[rows((i * 2 + z) * feat + p * (feat // 2), feat // 2), pl.ds(k * lanes, lanes)]

    spot = pq.at[rows((lax.rem(x, 2) * 2 + zl) * feat, feat), rows(c * lanes, lanes)]
    mark = (lax.rem(x, 2) * 2 + zl) * 2 + c
    at_home = (y == h) & (c == core)
    swap = remote(proj, spot, sw_s.at[0], pq_r.at[mark], dp_0=h, mp_0=y, mp_1=core)
    stay = pltpu.make_async_copy(proj, spot, pq_r.at[mark])

    @pl.when(jnp.logical_not(at_home))
    def _():
        swap.start()

    @pl.when(at_home)
    def _():
        stay.start()

    def slot(k, start, size):
        return inp4.at[k // 2, pl.ds((k % 2) * tok + start, size)]

    lo, hi = pl.ds(0, half), pl.ds(half, half)
    in_up = send(inp.at[lo], slot(1, 0, half), in_s.at[0], in_r.at[0], dp_0=up)
    in_dn = send(inp.at[hi], slot(3, half, half), in_s.at[1], in_r.at[1], dp_0=down)
    in_up2 = send(inp.at[hi], slot(1, half, half), in_s.at[2], in_r.at[2], dp_0=up)
    in_dn2 = send(inp.at[lo], slot(3, 0, half), in_s.at[3], in_r.at[3], dp_0=down)
    own_in = pltpu.make_async_copy(inp, slot(0, 0, tok), loc_sem.at[0])
    own_in.start()
    own_g = pltpu.make_async_copy(grads, ga.at[pl.ds(0, tok)], loc_sem.at[1])
    own_g.start()

    def away(i):
        return lax.rem(x + 4 - (2 * c + i), 4)

    later = []

    def ring(k, dz, stage):
        z = lax.rem(zl + dz, 2)
        for i in range(2):
            m = (i * 2 + z) * 2 + k
            whole = block(i, z, k)
            if stage == 0:
                fr = remote(whole, whole, ring_s.at[m, 0], pq_r.at[m], dp_1=right)
                fl = remote(whole, whole, ring_s.at[m, 1], pq_r.at[m], dp_1=left)
                both = (fr, fl)
                if dz == 0:
                    both = (remote(whole, whole, ring_s.at[m, 2], pq_r.at[m], dp_2=1 - zl), fr, fl)

                @pl.when(away(i) == 0)
                def _():
                    landed(whole, pq_r.at[m])
                    for cp in both:
                        cp.start()

                later.append((away(i) == 0, both))
            if stage == 1:
                for d, p, to in ((1, 0, right), (3, 1, left)):
                    some = part_of(i, z, k, p)
                    fw = remote(some, some, ring_s.at[m, p], ring_r.at[m, p], dp_1=to)

                    @pl.when(away(i) == d)
                    def _():
                        landed(whole, pq_r.at[m])
                        fw.start()

                    later.append((away(i) == d, (fw,)))
            if stage == 2:

                @pl.when(away(i) == 2)
                def _():
                    landed(part_of(i, z, k, 0), ring_r.at[m, 0])
                    landed(part_of(i, z, k, 1), ring_r.at[m, 1])

    ring(0, 0, 0)
    ring(1, 0, 0)
    in_up.wait_recv()
    fw_up = send(slot(1, 0, half), slot(2, 0, half), in_s.at[4], in_r.at[4], dp_0=up)
    in_dn.wait_recv()
    fw_dn = send(slot(3, half, half), slot(2, half, half), in_s.at[5], in_r.at[5], dp_0=down)
    ring(0, 1, 0)
    ring(1, 1, 0)

    def g_from(start, size):
        return ga.at[pl.ds(start, size)]

    g_up = send(grads.at[lo, pl.ds(0, wide)], g_from(tok, half), g_s.at[0], g_r.at[0], dp_0=up)
    g_dn = send(grads.at[hi, pl.ds(0, wide)], g_from(3 * tok + half, half), g_s.at[1], g_r.at[1], dp_0=down)
    g_up2 = send(grads.at[hi, pl.ds(0, wide)], g_from(tok + half, half), g_s.at[2], g_r.at[2], dp_0=up)
    g_dn2 = send(grads.at[lo, pl.ds(0, wide)], g_from(3 * tok, half), g_s.at[3], g_r.at[3], dp_0=down)
    for k in range(2):
        for dz in range(2):
            ring(k, dz, 1)
    own_in.wait()
    in_up2.wait_recv()
    in_dn2.wait_recv()
    fw_up.wait_recv()
    fw_dn.wait_recv()

    pairs = []
    for k in range(2):
        for dz in range(2):
            ring(k, dz, 2)
        out_half[k] = jnp.dot(
            inp4[1 - c], pq[:, pl.ds(k * lanes, lanes)], preferred_element_type=jnp.float32
        )
        pairs.append(send(out_half.at[k], half_in.at[k], half_s.at[k], half_r.at[k], mp_1=1 - c))
    for k in range(2):
        own[k] = jnp.dot(inp4[c], pq[:, pl.ds(k * lanes, lanes)], preferred_element_type=jnp.float32)

    cut = 2 * tok // 4
    q = cut // 2
    beyond = lax.rem(h + 2, 4)
    flow = {}

    def piece(k, of, p):
        return own.at[k, rows(of * cut + p * q, q)]

    def value(k, of, p):
        return own[k, rows(of * cut + p * q, q)]

    for k in range(2):
        pairs[k].wait_recv()
        own[k] += half_in[k]
        flow[k, 0] = send(piece(k, beyond, 0), via_d.at[k], rs_s.at[k, 0], rs_r.at[k, 0], mp_0=above)
        flow[k, 1] = send(piece(k, beyond, 1), via_u.at[k], rs_s.at[k, 1], rs_r.at[k, 1], mp_0=below)
        flow[k, 2] = send(piece(k, above, 1), raw_d.at[k], rs_s.at[k, 2], rs_r.at[k, 2], mp_0=above)
        flow[k, 3] = send(piece(k, below, 0), raw_u.at[k], rs_s.at[k, 3], rs_r.at[k, 3], mp_0=below)
    for k in range(2):
        flow[k, 0].wait_recv()
        turn_u[k] = via_d[k] + value(k, above, 0)
        flow[k, 4] = send(turn_u.at[k], add_d.at[k], rs_s.at[k, 4], rs_r.at[k, 4], mp_0=above)
        flow[k, 1].wait_recv()
        turn_d[k] = via_u[k] + value(k, below, 1)
        flow[k, 5] = send(turn_d.at[k], add_u.at[k], rs_s.at[k, 5], rs_r.at[k, 5], mp_0=below)

    def share(k, of, start=0, size=cut, who=c):
        return pa.at[rows(who * 2 * tok + of * cut + start, size, size), pl.ds(k * lanes, lanes)]

    for k in range(2):
        for i in (2, 3, 4, 5):
            flow[k, i].wait_recv()
        top = value(k, h, 0) + add_d[k] + raw_u[k]
        low = value(k, h, 1) + add_u[k] + raw_d[k]
        pa[rows(c * 2 * tok + h * cut, cut), pl.ds(k * lanes, lanes)] = jnp.concatenate(
            [top, low], axis=0
        ).astype(pa.dtype)
        flow[k, 6] = send(share(k, h), share(k, h), sh_s.at[k, 0], sh_r.at[k, 0], mp_0=above)
        flow[k, 7] = send(share(k, h), share(k, h), sh_s.at[k, 1], sh_r.at[k, 1], mp_0=below)
        send(share(k, h), share(k, h), sh_s.at[k, 4], sh_r.at[k, 4], mp_1=1 - c)
    g_up.wait_recv()
    gf_up = send(g_from(tok, half), g_from(2 * tok, half), g_s.at[4], g_r.at[4], dp_0=up)
    g_dn.wait_recv()
    gf_dn = send(
        g_from(3 * tok + half, half), g_from(2 * tok + half, half), g_s.at[5], g_r.at[5], dp_0=down
    )
    for k in range(2):
        landed(share(k, below), sh_r.at[k, 0])
        send(share(k, below, 0, q), share(k, below, 0, q), sh_s.at[k, 2], sh_r.at[k, 2], mp_0=above)
        send(share(k, below), share(k, below), sh_s.at[k, 5], sh_r.at[k, 5], mp_1=1 - c)
        landed(share(k, above), sh_r.at[k, 1])
        send(share(k, above, q, q), share(k, above, q, q), sh_s.at[k, 3], sh_r.at[k, 3], mp_0=below)
        send(share(k, above), share(k, above), sh_s.at[k, 6], sh_r.at[k, 6], mp_1=1 - c)
    for k in range(2):
        landed(share(k, beyond, 0, q), sh_r.at[k, 2])
        landed(share(k, beyond, q, q), sh_r.at[k, 3])
        send(share(k, beyond), share(k, beyond), sh_s.at[k, 7], sh_r.at[k, 7], mp_1=1 - c)
    for k in range(2):
        for i, of in enumerate((h, below, above, beyond)):
            landed(share(k, of, who=1 - c), sh_r.at[k, 4 + i])
    g_up2.wait_recv()
    g_dn2.wait_recv()
    gf_up.wait_recv()
    gf_dn.wait_recv()
    own_g.wait()

    def finish():
        for cp in sent:
            cp.wait_send()
        for when, copies in later + [(jnp.logical_not(at_home), (swap,))]:

            @pl.when(when)
            def _():
                for cp in copies:
                    cp.wait_send()

    return finish


def update_body(
    chunks, early, pa, ga, proj, new_first, new_second, full, prow,
    part, raw_l, raw_r, via_l, via_r, turn_r, turn_l, add_l, add_r, zsend, zrecv, both, stage, first_m, second_m,
    keep_sem, put_sem, rs_s, rs_r, d_s, d_r, ag_s, ag_r, p_s, p_r,
):
    y, x, zl, h, c = place()
    n = first_m.shape[0]
    lanes = proj.shape[1]
    f32 = jnp.float32
    right, left, far = lax.rem(x + 1, 4), lax.rem(x + 3, 4), lax.rem(x + 2, 4)

    def plus(at, d):
        return lax.rem(at + d, 4)

    sent = []
    flow = {}

    def send(name, src, dst, s, r, **where):
        cp = remote(src, dst, s, r, **where)
        cp.start()
        sent.append(cp)
        flow[name] = cp

    def cols(k):
        return pl.ds(chunks[k][0], chunks[k][1])

    def piece(k, of, half):
        return part.at[rows(of * 2 * n + half * n, n), cols(k)]

    def mine_of(k, start):
        return part[rows(start, n), cols(k)].astype(f32)

    def at(ref, k):
        return ref.at[:, cols(k)]

    def rs_far(k):
        send((k, 0), piece(k, far, 0), at(via_l, k), rs_s.at[k, 0], rs_r.at[k, 0], dp_1=right)
        send((k, 1), piece(k, far, 1), at(via_r, k), rs_s.at[k, 1], rs_r.at[k, 1], dp_1=left)

    def rs_near(k):
        send((k, 2), piece(k, right, 1), at(raw_l, k), rs_s.at[k, 2], rs_r.at[k, 2], dp_1=right)
        send((k, 3), piece(k, left, 0), at(raw_r, k), rs_s.at[k, 3], rs_r.at[k, 3], dp_1=left)

    def load(ref, k, where=slice(None)):
        return ref[where, cols(k)].astype(f32)

    def rs_turn(k):
        flow[k, 0].wait_recv()
        turn_r[:, cols(k)] = (load(via_l, k) + mine_of(k, right * 2 * n)).astype(turn_r.dtype)
        send((k, 4), at(turn_r, k), at(add_l, k), rs_s.at[k, 4], rs_r.at[k, 4], dp_1=right)
        flow[k, 1].wait_recv()
        turn_l[:, cols(k)] = (load(via_r, k) + mine_of(k, left * 2 * n + n)).astype(turn_l.dtype)
        send((k, 5), at(turn_l, k), at(add_r, k), rs_s.at[k, 5], rs_r.at[k, 5], dp_1=left)

    def total(k, half):
        if half == 0:
            return mine_of(k, x * 2 * n) + load(add_l, k) + load(raw_r, k)
        return mine_of(k, x * 2 * n + n) + load(add_r, k) + load(raw_l, k)

    def rs_sum(k):
        for i in (2, 3, 4, 5):
            flow[k, i].wait_recv()
        for mine in range(2):

            @pl.when(zl == mine)
            def _():
                zsend[:, cols(k)] = total(k, 1 - mine).astype(zsend.dtype)

        send((k, 6), at(zsend, k), at(zrecv, k), rs_s.at[k, 6], rs_r.at[k, 6], dp_2=1 - zl)
        for mine in range(2):

            @pl.when(zl == mine)
            def _():
                new_first[:, cols(k)] = total(k, mine)

    def adam(k):
        flow[k, 6].wait_recv()
        grad = new_first[:, cols(k)] + load(zrecv, k)
        m1 = 0.9 * first_m[:, cols(k)] + 0.1 * grad
        m2 = 0.999 * second_m[:, cols(k)] + 0.001 * grad * grad
        new_first[:, cols(k)] = m1
        new_second[:, cols(k)] = m2
        first_fix = 1.0 - 0.9**STEP
        second_fix = 1.0 - 0.999**STEP
        both[rows(zl * n, n), cols(k)] = (
            m1 / first_fix / (jnp.sqrt(m2 / second_fix) + 1e-08)
        ).astype(both.dtype)
        own = both.at[rows(zl * n, n), cols(k)]
        if not crossing(k):
            send((k, "d"), own, own, d_s.at[k], d_r.at[k], dp_2=1 - zl)

    def crossing(k):
        return chunks[k][3]

    def line(k):
        if chunks[k][2] == 0:
            return "dp_1", "dp_0", x, y, 1, 4
        return "dp_0", "dp_1", y, x, 4, 1

    def deep(k):
        return n if crossing(k) else 2 * n

    def region(k, p1, p2, start, size, z=zl):
        f1, f2 = line(k)[4:]
        if crossing(k):
            start = start + z * n
        return full.at[rows((p1 * f1 + p2 * f2) * 2 * n + start, size, n // 2), cols(k)]

    def whole(k, p1, p2, z=zl):
        return region(k, p1, p2, 0, deep(k), z)

    def side(k, p1, p2, half):
        size = deep(k) // 2
        return region(k, p1, p2, half * size, size)

    def pass_on(k, i, axis, to, where, src=None):
        send((k, "a", i), where if src is None else src, where, ag_s.at[k, i], ag_r.at[k, i], **{axis: to})

    def cross(k, d1, d2, src=None):
        if crossing(k):
            at1, at2 = line(k)[2:4]
            where, i = whole(k, plus(at1, d1), plus(at2, d2)), 20 + d1 * 4 + d2
            send((k, "a", i), where if src is None else src, where, ag_s.at[k, i], ag_r.at[k, i], dp_2=1 - zl)

    def ag_own(k):
        first, second, at1, at2 = line(k)[:4]
        if crossing(k):
            src = both.at[rows(zl * n, n), cols(k)]
        else:
            landed(both.at[rows((1 - zl) * n, n), cols(k)], d_r.at[k])
            src = both.at[:, cols(k)]
        here = whole(k, at1, at2)
        pass_on(k, 0, first, plus(at1, 1), here, src)
        pass_on(k, 1, first, plus(at1, 3), here, src)
        pass_on(k, 4, second, plus(at2, 1), here, src)
        pass_on(k, 8, second, plus(at2, 3), here, src)
        cross(k, 0, 0, src)
        pltpu.make_async_copy(src, here, put_sem.at[k]).start()

    def ag_first(k):
        first, second, at1, at2 = line(k)[:4]
        for j, d, to in ((0, 3, 1), (1, 1, 3)):
            here = whole(k, plus(at1, d), at2)
            landed(here, ag_r.at[k, j])
            pass_on(k, 2 + j, first, plus(at1, to), side(k, plus(at1, d), at2, j))
            pass_on(k, 5 + j, second, plus(at2, 1), here)
            pass_on(k, 9 + j, second, plus(at2, 3), here)
            cross(k, d, 0)

    def ag_far(k):
        first, second, at1, at2 = line(k)[:4]
        landed(side(k, plus(at1, 2), at2, 0), ag_r.at[k, 2])
        landed(side(k, plus(at1, 2), at2, 1), ag_r.at[k, 3])
        here = whole(k, plus(at1, 2), at2)
        pass_on(k, 7, second, plus(at2, 1), here)
        pass_on(k, 11, second, plus(at2, 3), here)
        cross(k, 2, 0)

    def ag_second(k, i):
        first, second, at1, at2 = line(k)[:4]
        d = (0, 3, 1, 2)[i]
        landed(whole(k, plus(at1, d), plus(at2, 3)), ag_r.at[k, 4 + i])
        pass_on(k, 12 + i, second, plus(at2, 1), side(k, plus(at1, d), plus(at2, 3), 0))
        cross(k, d, 3)
        landed(whole(k, plus(at1, d), plus(at2, 1)), ag_r.at[k, 8 + i])
        pass_on(k, 16 + i, second, plus(at2, 3), side(k, plus(at1, d), plus(at2, 1), 1))
        cross(k, d, 1)

    def ag_last(k, i):
        first, second, at1, at2 = line(k)[:4]
        d = (0, 3, 1, 2)[i]
        landed(side(k, plus(at1, d), plus(at2, 2), 0), ag_r.at[k, 12 + i])
        landed(side(k, plus(at1, d), plus(at2, 2), 1), ag_r.at[k, 16 + i])
        cross(k, d, 2)

    def ag_end(k):
        first, second, at1, at2 = line(k)[:4]
        if crossing(k):
            for d1 in range(4):
                for d2 in range(4):
                    landed(whole(k, plus(at1, d1), plus(at2, d2), 1 - zl), ag_r.at[k, 20 + d1 * 4 + d2])
        landed(whole(k, at1, at2), put_sem.at[k])

    above, below, beyond = plus(h, 1), plus(h, 3), plus(h, 2)
    tall = proj.shape[0] // 2

    def strip(of, who=c):
        return prow.at[:, rows((of * 2 + who) * lanes, lanes)]

    def bit(of, p):
        return prow.at[pl.ds(p * tall, tall), rows((of * 2 + c) * lanes, lanes)]

    def to_core(i, of, src=None):
        send(("p", i), strip(of) if src is None else src, strip(of), p_s.at[i], p_r.at[i], mp_1=1 - c)

    def rows_own():
        take.wait()
        keep.start()
        send(("p", 0), stage, strip(h), p_s.at[0], p_r.at[0], mp_0=above)
        send(("p", 1), stage, strip(h), p_s.at[1], p_r.at[1], mp_0=below)
        to_core(4, h, stage)

    def rows_on():
        landed(strip(below), p_r.at[0])
        send(("p", 2), bit(below, 0), bit(below, 0), p_s.at[2], p_r.at[2], mp_0=above)
        landed(strip(above), p_r.at[1])
        send(("p", 3), bit(above, 1), bit(above, 1), p_s.at[3], p_r.at[3], mp_0=below)
        to_core(5, below)
        to_core(6, above)

    def rows_far():
        landed(bit(beyond, 0), p_r.at[2])
        landed(bit(beyond, 1), p_r.at[3])
        to_core(7, beyond)

    def rows_end():
        for i, of in enumerate((h, below, above, beyond)):
            landed(strip(of, 1 - c), p_r.at[4 + i])
        keep.wait()

    take, *state = early
    keep = pltpu.make_async_copy(stage, strip(h), keep_sem)

    def dots(k):
        part[:, cols(k)] = lax.dot_general(
            pa[...], ga[:, cols(k)], (((0,), (0,)), ((), ())), preferred_element_type=f32
        ).astype(part.dtype)

    dots(0)
    rs_far(0)
    rs_near(0)
    dots(1)
    rs_far(1)
    rs_turn(0)
    rs_near(1)
    dots(2)
    rs_far(2)
    rows_own()
    rs_sum(0)
    rs_turn(1)
    rs_near(2)
    dots(3)
    rs_far(3)
    for cp in state:
        cp.wait()
    adam(0)
    ag_own(0)
    rs_sum(1)
    rs_turn(2)
    rs_near(3)
    adam(1)
    ag_own(1)
    ag_first(0)
    rs_sum(2)
    rs_turn(3)
    ag_far(0)
    adam(2)
    rs_sum(3)
    ag_first(1)
    ag_own(2)
    rows_on()
    adam(3)
    ag_second(0, 0)
    ag_far(1)
    ag_own(3)
    ag_second(0, 1)
    ag_first(2)
    ag_second(0, 2)
    ag_second(0, 3)
    ag_first(3)
    for i in range(4):
        ag_last(0, i)
    rows_far()
    ag_far(2)
    ag_far(3)
    for i in range(4):
        for k in (1, 2, 3):
            ag_second(k, i)
    for i in range(4):
        for k in (1, 2, 3):
            ag_last(k, i)
    for k in range(4):
        ag_end(k)
    rows_end()
    for cp in sent:
        cp.wait_send()


def split(cols):
    tiles = cols // 128
    first, second, third = tiles * 4 // 26, tiles * 6 // 26, tiles * 8 // 26
    ends = (0, first, first + second, first + second + third, tiles)
    kinds = ((0, True), (0, True), (0, False), (1, False))
    return tuple((128 * a, 128 * (b - a), *kind) for a, b, kind in zip(ends, ends[1:], kinds))


def step_kernel(
    chunks, inp, proj, grads, first_in, second_in, new_first, new_second, full, prow,
    pa, ga, part, stage, first_m, second_m, early_sem, *rest
):
    y, x, zl, h, c = place()
    peers = [{"mp_1": 1 - c}, {"dp_2": 1 - zl}]
    for axis, at in (("dp_0", y), ("dp_1", x), ("mp_0", h)):
        peers += [{axis: lax.rem(at + 1, 4)}, {axis: lax.rem(at + 3, 4)}]
    peers.append({"dp_0": h, "mp_0": y, "mp_1": 1 - c})
    early = [
        pltpu.make_async_copy(src, dst, early_sem.at[i])
        for i, (src, dst) in enumerate(((proj, stage), (first_in, first_m), (second_in, second_m)))
    ]
    for cp in early:
        cp.start()
    greet(peers, ({"dp_0": h, "mp_0": y}, y != h))
    bufs1, rest = rest[:13], rest[13:]
    sems1, rest = rest[:15], rest[15:]
    bufs2, sems2 = rest[:11], rest[11:]
    finish = projected_body(inp, proj, grads, pa, ga, *bufs1, *sems1)
    update_body(
        chunks, early, pa, ga, proj, new_first, new_second, full, prow,
        part, *bufs2, stage, first_m, second_m, *sems2,
    )
    finish()


def step(inputs, projector, out_grads, first_moment, second_moment):
    tok, feats = inputs.shape
    feat, lanes = projector.shape
    n, cols = first_moment.shape
    bf, f32 = jnp.bfloat16, jnp.float32
    small = pltpu.VMEM((2, tok // 4, lanes), f32)
    slot = pltpu.VMEM((n, cols), bf)
    chunks = split(cols)
    count = len(chunks)
    return pl.pallas_call(
        functools.partial(step_kernel, chunks),
        name="step",
        out_shape=(
            jax.ShapeDtypeStruct((n, cols), f32),
            jax.ShapeDtypeStruct((n, cols), f32),
            jax.ShapeDtypeStruct((32 * n, cols), bf),
            jax.ShapeDtypeStruct((feat, 8 * lanes), bf),
        ),
        in_specs=[ANY] * 5,
        out_specs=(VMEM, VMEM, ANY, ANY),
        scratch_shapes=[
            pltpu.VMEM((4 * tok, 2 * lanes), bf),
            pltpu.VMEM((4 * tok, cols), bf),
            pltpu.VMEM((8 * n, cols), bf),
            pltpu.VMEM((feat, lanes), bf),
            pltpu.VMEM((n, cols), f32),
            pltpu.VMEM((n, cols), f32),
            DMA((3,)),
            pltpu.VMEM((2, 2 * tok, feats), bf),
            pltpu.VMEM((4 * feat, 2 * lanes), bf),
            pltpu.VMEM((2, 2 * tok, lanes), f32),
            pltpu.VMEM((2, 2 * tok, lanes), f32),
            pltpu.VMEM((2, 2 * tok, lanes), f32),
            *[small] * 8,
            DMA((2,)),
            DMA((6,)), DMA((6,)),
            DMA((6,)), DMA((6,)),
            DMA((1,)), DMA((8,)),
            DMA((8, 3)), DMA((8, 2)),
            DMA((2,)), DMA((2,)),
            DMA((2, 6)), DMA((2, 6)),
            DMA((2, 8)), DMA((2, 8)),
            *[slot] * 10,
            pltpu.VMEM((2 * n, cols), bf),
            DMA,
            DMA((count,)),
            DMA((count, 7)), DMA((count, 7)),
            DMA((count,)), DMA((count,)),
            DMA((count, 36)), DMA((count, 36)),
            DMA((8,)), DMA((8,)),
        ],
        compiler_params=pltpu.CompilerParams(
            collective_id=0, has_side_effects=True, vmem_limit_bytes=24 << 20
        ),
    )(*(in_hbm(v) for v in (inputs, projector, out_grads, first_moment, second_moment)))


def per_device(inputs, projector, out_grads, weights, first_moment, second_moment):
    new_first, new_second, full, ranks = step(
        inputs, projector, out_grads, first_moment, second_moment
    )
    lifted = jnp.dot(ranks, full, preferred_element_type=jnp.float32)
    new_weights = (weights.astype(jnp.float32) - 2.0 * lifted).astype(jnp.bfloat16)
    return (new_weights, new_first, new_second)


def solution(mesh):
    finer = Mesh(mesh.devices.reshape(4, 4, 2, 4, 2), AXES)
    spec = P(DP, MP)
    return jax.shard_map(
        per_device, mesh=finer, in_specs=(spec,) * 6, out_specs=(spec,) * 3, check_vma=False
    )
```

```python
import functools

import jax
import jax.numpy as jnp
from jax import lax
from jax.experimental import pallas as pl
from jax.experimental.pallas import tpu as pltpu
from jax.sharding import Mesh
from jax.sharding import PartitionSpec as P

STEP = 1000
AXES = ("dp_0", "dp_1", "dp_2", "mp_0", "mp_1")
DP = AXES[:3]
MP = AXES[3:]
MESH = pl.DeviceIdType.MESH
ANY = pl.BlockSpec(memory_space=pl.ANY)
VMEM = pl.BlockSpec(memory_space=pltpu.VMEM)
DMA = pltpu.SemaphoreType.DMA


ORDER = (
    ('dots', 0), ('far', 0), ('dots', 1), ('far', 1), ('dots', 2), ('far', 2), ('dots', 3), ('far', 3),
    ('dots', 4), ('far', 4), ('near', 0), ('near', 1), ('near', 2), ('near', 3), ('near', 4), ('turn', 0),
    ('turn', 1), ('turn', 2), ('turn', 3), ('turn', 4), ('sum', 0), ('sum', 1), ('sum', 2), ('adam', 0),
    ('sum', 3), ('adam', 1), ('rows_on',), ('own', 1), ('sum', 4), ('adam', 2), ('own', 2), ('own', 0),
    ('first', 1, 0), ('adam', 3), ('first', 1, 1), ('second', 1, 0, 0), ('second', 1, 0, 1), ('first', 2, 0),
    ('first', 2, 1), ('second', 2, 0, 0), ('second', 2, 0, 1), ('adam', 4), ('first', 0, 0), ('first', 0, 1),
    ('second', 0, 0, 0), ('second', 0, 0, 1), ('farg', 1), ('rows_far',), ('second', 1, 1, 0),
    ('second', 1, 1, 1), ('second', 1, 2, 0), ('second', 1, 2, 1), ('last', 1, 0), ('farg', 2), ('own', 3),
    ('second', 2, 1, 0), ('second', 2, 1, 1), ('second', 0, 1, 0), ('second', 0, 1, 1), ('second', 2, 2, 0),
    ('second', 2, 2, 1), ('last', 2, 0), ('second', 0, 2, 0), ('farg', 0), ('second', 0, 2, 1),
    ('last', 0, 0), ('second', 1, 3, 0), ('second', 1, 3, 1), ('last', 1, 1), ('last', 1, 2),
    ('second', 2, 3, 0), ('second', 2, 3, 1), ('second', 3, 0, 0), ('second', 3, 0, 1), ('last', 0, 1),
    ('second', 0, 3, 1), ('own', 4), ('first', 3, 0), ('second', 0, 3, 0), ('last', 0, 2), ('first', 3, 1),
    ('last', 2, 1), ('last', 2, 2), ('last', 1, 3), ('last', 3, 0), ('last', 2, 3), ('first', 4, 0),
    ('second', 4, 0, 0), ('first', 4, 1), ('second', 4, 0, 1), ('farg', 3), ('second', 3, 1, 0),
    ('second', 3, 1, 1), ('last', 0, 3), ('end', 0), ('second', 4, 1, 0), ('second', 4, 1, 1),
    ('second', 3, 2, 1), ('second', 3, 2, 0), ('second', 4, 2, 1), ('farg', 4), ('second', 4, 2, 0),
    ('last', 4, 0), ('last', 4, 1), ('second', 3, 3, 1), ('second', 3, 3, 0), ('second', 4, 3, 0),
    ('last', 3, 1), ('second', 4, 3, 1), ('end', 1), ('last', 4, 2), ('last', 3, 2), ('end', 2),
    ('last', 3, 3), ('end', 3), ('last', 4, 3), ('end', 4), ('rows_end',),
)


def in_hbm(x):
    return pltpu.with_memory_space_constraint(x, pltpu.HBM)


def place():
    return tuple(lax.axis_index(a) for a in AXES)


def remote(src, dst, send_sem, recv_sem, **where):
    return pltpu.make_async_remote_copy(
        src_ref=src,
        dst_ref=dst,
        send_sem=send_sem,
        recv_sem=recv_sem,
        device_id=where,
        device_id_type=MESH,
    )


def landed(dst, sem):
    pltpu.make_async_copy(dst, dst, sem).wait()


def rows(start, size, unit=None):
    return pl.ds(pl.multiple_of(start, unit or size), size)


def greet(peers, extra=None):
    barrier = pltpu.get_barrier_semaphore()
    for peer in peers:
        pl.semaphore_signal(barrier, inc=1, device_id=peer, device_id_type=MESH)
    count = len(peers)
    if extra is not None:
        peer, present = extra

        @pl.when(present)
        def _():
            pl.semaphore_signal(barrier, inc=1, device_id=peer, device_id_type=MESH)

        count = count + present.astype(jnp.int32)
    pl.semaphore_wait(barrier, count)


def projected_body(
    inp, proj, grads, pa, ga,
    inp4, pq, own, out_half, half_in, via_d, via_u, raw_d, raw_u, turn_u, turn_d, add_d, add_u,
    rows_own, loc_sem, in_s, in_r, g_s, g_r, sw_s, pq_r, ring_s, ring_r, half_s, half_r, rs_s, rs_r, sh_s, sh_r,
):
    y, x, zl, h, c = place()
    up, down = lax.rem(y + 1, 4), lax.rem(y + 3, 4)
    right, left = lax.rem(x + 1, 4), lax.rem(x + 3, 4)
    above, below = lax.rem(h + 1, 4), lax.rem(h + 3, 4)
    tok = inp.shape[0]
    half = tok // 2
    feat, lanes = proj.shape
    wide = ga.shape[1]
    sent = []

    def send(src, dst, s, r, **where):
        cp = remote(src, dst, s, r, **where)
        cp.start()
        sent.append(cp)
        return cp

    core = x // 2

    def block(i, z, k):
        return pq.at[rows((i * 2 + z) * feat, feat), pl.ds(k * lanes, lanes)]

    def part_of(i, z, k, p):
        return pq.at[rows((i * 2 + z) * feat + p * (feat // 2), feat // 2), pl.ds(k * lanes, lanes)]

    spot = pq.at[rows((lax.rem(x, 2) * 2 + zl) * feat, feat), rows(c * lanes, lanes)]
    mark = (lax.rem(x, 2) * 2 + zl) * 2 + c
    at_home = (y == h) & (c == core)
    swap = remote(proj, spot, sw_s.at[0], pq_r.at[mark], dp_0=h, mp_0=y, mp_1=core)
    stay = pltpu.make_async_copy(proj, spot, pq_r.at[mark])

    @pl.when(jnp.logical_not(at_home))
    def _():
        swap.start()

    @pl.when(at_home)
    def _():
        stay.start()

    def slot(k, start, size):
        return inp4.at[k // 2, pl.ds((k % 2) * tok + start, size)]

    lo, hi = pl.ds(0, half), pl.ds(half, half)
    in_up = send(inp.at[lo], slot(1, 0, half), in_s.at[0], in_r.at[0], dp_0=up)
    in_dn = send(inp.at[hi], slot(3, half, half), in_s.at[1], in_r.at[1], dp_0=down)
    in_up2 = send(inp.at[hi], slot(1, half, half), in_s.at[2], in_r.at[2], dp_0=up)
    in_dn2 = send(inp.at[lo], slot(3, 0, half), in_s.at[3], in_r.at[3], dp_0=down)
    own_in = pltpu.make_async_copy(inp, slot(0, 0, tok), loc_sem.at[0])
    own_in.start()
    own_g = pltpu.make_async_copy(grads, ga.at[pl.ds(0, tok)], loc_sem.at[1])
    own_g.start()

    def away(i):
        return lax.rem(x + 4 - (2 * c + i), 4)

    later = []

    def ring(k, dz, stage):
        z = lax.rem(zl + dz, 2)
        for i in range(2):
            m = (i * 2 + z) * 2 + k
            whole = block(i, z, k)
            if stage == 0:
                fr = remote(whole, whole, ring_s.at[m, 0], pq_r.at[m], dp_1=right)
                fl = remote(whole, whole, ring_s.at[m, 1], pq_r.at[m], dp_1=left)
                both = (fr, fl)
                if dz == 0:
                    both = (remote(whole, whole, ring_s.at[m, 2], pq_r.at[m], dp_2=1 - zl), fr, fl)

                @pl.when(away(i) == 0)
                def _():
                    landed(whole, pq_r.at[m])
                    for cp in both:
                        cp.start()

                later.append((away(i) == 0, both))
            if stage == 1:
                for d, p, to in ((1, 0, right), (3, 1, left)):
                    some = part_of(i, z, k, p)
                    fw = remote(some, some, ring_s.at[m, p], ring_r.at[m, p], dp_1=to)

                    @pl.when(away(i) == d)
                    def _():
                        landed(whole, pq_r.at[m])
                        fw.start()

                    later.append((away(i) == d, (fw,)))
            if stage == 2:

                @pl.when(away(i) == 2)
                def _():
                    landed(part_of(i, z, k, 0), ring_r.at[m, 0])
                    landed(part_of(i, z, k, 1), ring_r.at[m, 1])

    ring(0, 0, 0)
    ring(1, 0, 0)
    in_up.wait_recv()
    fw_up = send(slot(1, 0, half), slot(2, 0, half), in_s.at[4], in_r.at[4], dp_0=up)
    in_dn.wait_recv()
    fw_dn = send(slot(3, half, half), slot(2, half, half), in_s.at[5], in_r.at[5], dp_0=down)
    ring(0, 1, 0)
    ring(1, 1, 0)

    def g_from(start, size):
        return ga.at[pl.ds(start, size)]

    g_up = send(grads.at[lo, pl.ds(0, wide)], g_from(tok, half), g_s.at[0], g_r.at[0], dp_0=up)
    g_dn = send(grads.at[hi, pl.ds(0, wide)], g_from(3 * tok + half, half), g_s.at[1], g_r.at[1], dp_0=down)
    g_up2 = send(grads.at[hi, pl.ds(0, wide)], g_from(tok + half, half), g_s.at[2], g_r.at[2], dp_0=up)
    g_dn2 = send(grads.at[lo, pl.ds(0, wide)], g_from(3 * tok, half), g_s.at[3], g_r.at[3], dp_0=down)
    for k in range(2):
        for dz in range(2):
            ring(k, dz, 1)
    own_in.wait()
    in_up2.wait_recv()
    in_dn2.wait_recv()
    fw_up.wait_recv()
    fw_dn.wait_recv()

    pairs = []
    for k in range(2):
        for dz in range(2):
            ring(k, dz, 2)
        out_half[k] = jnp.dot(
            inp4[1 - c], pq[:, pl.ds(k * lanes, lanes)], preferred_element_type=jnp.float32
        )
        pairs.append(send(out_half.at[k], half_in.at[k], half_s.at[k], half_r.at[k], mp_1=1 - c))
    for k in range(2):
        own[k] = jnp.dot(inp4[c], pq[:, pl.ds(k * lanes, lanes)], preferred_element_type=jnp.float32)

    cut = 2 * tok // 4
    q = cut // 2
    beyond = lax.rem(h + 2, 4)
    flow = {}

    def piece(k, of, p):
        return own.at[k, rows(of * cut + p * q, q)]

    def value(k, of, p):
        return own[k, rows(of * cut + p * q, q)]

    for k in range(2):
        pairs[k].wait_recv()
        own[k] += half_in[k]
        flow[k, 0] = send(piece(k, beyond, 0), via_d.at[k], rs_s.at[k, 0], rs_r.at[k, 0], mp_0=above)
        flow[k, 1] = send(piece(k, beyond, 1), via_u.at[k], rs_s.at[k, 1], rs_r.at[k, 1], mp_0=below)
        flow[k, 2] = send(piece(k, above, 1), raw_d.at[k], rs_s.at[k, 2], rs_r.at[k, 2], mp_0=above)
        flow[k, 3] = send(piece(k, below, 0), raw_u.at[k], rs_s.at[k, 3], rs_r.at[k, 3], mp_0=below)
    for k in range(2):
        flow[k, 0].wait_recv()
        turn_u[k] = via_d[k] + value(k, above, 0)
        flow[k, 4] = send(turn_u.at[k], add_d.at[k], rs_s.at[k, 4], rs_r.at[k, 4], mp_0=above)
        flow[k, 1].wait_recv()
        turn_d[k] = via_u[k] + value(k, below, 1)
        flow[k, 5] = send(turn_d.at[k], add_u.at[k], rs_s.at[k, 5], rs_r.at[k, 5], mp_0=below)

    def share(k, of, start=0, size=cut, who=c):
        return pa.at[rows(who * 2 * tok + of * cut + start, size, size), pl.ds(k * lanes, lanes)]

    for k in range(2):
        for i in (2, 3, 4, 5):
            flow[k, i].wait_recv()
        top = value(k, h, 0) + add_d[k] + raw_u[k]
        low = value(k, h, 1) + add_u[k] + raw_d[k]
        pa[rows(c * 2 * tok + h * cut, cut), pl.ds(k * lanes, lanes)] = jnp.concatenate(
            [top, low], axis=0
        ).astype(pa.dtype)
        flow[k, 6] = send(share(k, h), share(k, h), sh_s.at[k, 0], sh_r.at[k, 0], mp_0=above)
        flow[k, 7] = send(share(k, h), share(k, h), sh_s.at[k, 1], sh_r.at[k, 1], mp_0=below)
        send(share(k, h), share(k, h), sh_s.at[k, 4], sh_r.at[k, 4], mp_1=1 - c)
    g_up.wait_recv()
    gf_up = send(g_from(tok, half), g_from(2 * tok, half), g_s.at[4], g_r.at[4], dp_0=up)
    g_dn.wait_recv()
    gf_dn = send(
        g_from(3 * tok + half, half), g_from(2 * tok + half, half), g_s.at[5], g_r.at[5], dp_0=down
    )
    for k in range(2):
        landed(share(k, below), sh_r.at[k, 0])
        send(share(k, below, 0, q), share(k, below, 0, q), sh_s.at[k, 2], sh_r.at[k, 2], mp_0=above)
        send(share(k, below), share(k, below), sh_s.at[k, 5], sh_r.at[k, 5], mp_1=1 - c)
        landed(share(k, above), sh_r.at[k, 1])
        send(share(k, above, q, q), share(k, above, q, q), sh_s.at[k, 3], sh_r.at[k, 3], mp_0=below)
        send(share(k, above), share(k, above), sh_s.at[k, 6], sh_r.at[k, 6], mp_1=1 - c)
    for k in range(2):
        landed(share(k, beyond, 0, q), sh_r.at[k, 2])
        landed(share(k, beyond, q, q), sh_r.at[k, 3])
        send(share(k, beyond), share(k, beyond), sh_s.at[k, 7], sh_r.at[k, 7], mp_1=1 - c)
    rows_own()
    for k in range(2):
        for i, of in enumerate((h, below, above, beyond)):
            landed(share(k, of, who=1 - c), sh_r.at[k, 4 + i])
    g_up2.wait_recv()
    g_dn2.wait_recv()
    gf_up.wait_recv()
    gf_dn.wait_recv()
    own_g.wait()

    def finish():
        for cp in sent:
            cp.wait_send()
        for when, copies in later + [(jnp.logical_not(at_home), (swap,))]:

            @pl.when(when)
            def _():
                for cp in copies:
                    cp.wait_send()

    return finish


def update_body(
    chunks, early, pa, ga, proj, new_first, new_second, full, prow,
    part, raw_l, raw_r, via_l, via_r, turn_r, turn_l, add_l, add_r, zsend, zrecv, both, stage, first_m, second_m,
    keep_sem, put_sem, rs_s, rs_r, d_s, d_r, ag_s, ag_r, p_s, p_r,
):
    y, x, zl, h, c = place()
    n = first_m.shape[0]
    lanes = proj.shape[1]
    f32 = jnp.float32
    right, left, far = lax.rem(x + 1, 4), lax.rem(x + 3, 4), lax.rem(x + 2, 4)

    def plus(at, d):
        return lax.rem(at + d, 4)

    sent = []
    flow = {}

    def send(name, src, dst, s, r, **where):
        cp = remote(src, dst, s, r, **where)
        cp.start()
        sent.append(cp)
        flow[name] = cp

    def cols(k):
        return pl.ds(chunks[k][0], chunks[k][1])

    def piece(k, of, half):
        return part.at[rows(of * 2 * n + half * n, n), cols(k)]

    def mine_of(k, start):
        return part[rows(start, n), cols(k)].astype(f32)

    def at(ref, k):
        return ref.at[:, cols(k)]

    def rs_far(k):
        send((k, 0), piece(k, far, 0), at(via_l, k), rs_s.at[k, 0], rs_r.at[k, 0], dp_1=right)
        send((k, 1), piece(k, far, 1), at(via_r, k), rs_s.at[k, 1], rs_r.at[k, 1], dp_1=left)

    def rs_near(k):
        send((k, 2), piece(k, right, 1), at(raw_l, k), rs_s.at[k, 2], rs_r.at[k, 2], dp_1=right)
        send((k, 3), piece(k, left, 0), at(raw_r, k), rs_s.at[k, 3], rs_r.at[k, 3], dp_1=left)

    def load(ref, k, where=slice(None)):
        return ref[where, cols(k)].astype(f32)

    def rs_turn(k):
        flow[k, 0].wait_recv()
        turn_r[:, cols(k)] = (load(via_l, k) + mine_of(k, right * 2 * n)).astype(turn_r.dtype)
        send((k, 4), at(turn_r, k), at(add_l, k), rs_s.at[k, 4], rs_r.at[k, 4], dp_1=right)
        flow[k, 1].wait_recv()
        turn_l[:, cols(k)] = (load(via_r, k) + mine_of(k, left * 2 * n + n)).astype(turn_l.dtype)
        send((k, 5), at(turn_l, k), at(add_r, k), rs_s.at[k, 5], rs_r.at[k, 5], dp_1=left)

    def total(k, half):
        if half == 0:
            return mine_of(k, x * 2 * n) + load(add_l, k) + load(raw_r, k)
        return mine_of(k, x * 2 * n + n) + load(add_r, k) + load(raw_l, k)

    def rs_sum(k):
        for i in (2, 3, 4, 5):
            flow[k, i].wait_recv()
        for mine in range(2):

            @pl.when(zl == mine)
            def _():
                zsend[:, cols(k)] = total(k, 1 - mine).astype(zsend.dtype)

        send((k, 6), at(zsend, k), at(zrecv, k), rs_s.at[k, 6], rs_r.at[k, 6], dp_2=1 - zl)
        for mine in range(2):

            @pl.when(zl == mine)
            def _():
                new_first[:, cols(k)] = total(k, mine)

    def adam(k):
        flow[k, 6].wait_recv()
        grad = new_first[:, cols(k)] + load(zrecv, k)
        m1 = 0.9 * first_m[:, cols(k)] + 0.1 * grad
        m2 = 0.999 * second_m[:, cols(k)] + 0.001 * grad * grad
        new_first[:, cols(k)] = m1
        new_second[:, cols(k)] = m2
        first_fix = 1.0 - 0.9**STEP
        second_fix = 1.0 - 0.999**STEP
        both[rows(zl * n, n), cols(k)] = (
            m1 / first_fix / (jnp.sqrt(m2 / second_fix) + 1e-08)
        ).astype(both.dtype)
        own = both.at[rows(zl * n, n), cols(k)]
        if not crossing(k):
            send((k, "d"), own, own, d_s.at[k], d_r.at[k], dp_2=1 - zl)

    def crossing(k):
        return chunks[k][3]

    def line(k):
        if chunks[k][2] == 0:
            return "dp_1", "dp_0", x, y, 1, 4
        return "dp_0", "dp_1", y, x, 4, 1

    def deep(k):
        return n if crossing(k) else 2 * n

    def region(k, p1, p2, start, size, z=zl):
        f1, f2 = line(k)[4:]
        if crossing(k):
            start = start + z * n
        return full.at[rows((p1 * f1 + p2 * f2) * 2 * n + start, size, n // 2), cols(k)]

    def whole(k, p1, p2, z=zl):
        return region(k, p1, p2, 0, deep(k), z)

    def side(k, p1, p2, half):
        size = deep(k) // 2
        return region(k, p1, p2, half * size, size)

    def pass_on(k, i, axis, to, where, src=None):
        send((k, "a", i), where if src is None else src, where, ag_s.at[k, i], ag_r.at[k, i], **{axis: to})

    def cross(k, d1, d2, src=None):
        if crossing(k):
            at1, at2 = line(k)[2:4]
            where, i = whole(k, plus(at1, d1), plus(at2, d2)), 20 + d1 * 4 + d2
            send((k, "a", i), where if src is None else src, where, ag_s.at[k, i], ag_r.at[k, i], dp_2=1 - zl)

    def ag_own(k):
        first, second, at1, at2 = line(k)[:4]
        if crossing(k):
            src = both.at[rows(zl * n, n), cols(k)]
        else:
            landed(both.at[rows((1 - zl) * n, n), cols(k)], d_r.at[k])
            src = both.at[:, cols(k)]
        here = whole(k, at1, at2)
        pass_on(k, 0, first, plus(at1, 1), here, src)
        pass_on(k, 1, first, plus(at1, 3), here, src)
        pass_on(k, 4, second, plus(at2, 1), here, src)
        pass_on(k, 8, second, plus(at2, 3), here, src)
        cross(k, 0, 0, src)
        pltpu.make_async_copy(src, here, put_sem.at[k]).start()

    def ag_first(k, j):
        first, second, at1, at2 = line(k)[:4]
        d, to = ((3, 1), (1, 3))[j]
        here = whole(k, plus(at1, d), at2)
        landed(here, ag_r.at[k, j])
        pass_on(k, 2 + j, first, plus(at1, to), side(k, plus(at1, d), at2, j))
        pass_on(k, 5 + j, second, plus(at2, 1), here)
        pass_on(k, 9 + j, second, plus(at2, 3), here)
        cross(k, d, 0)

    def ag_far(k):
        first, second, at1, at2 = line(k)[:4]
        landed(side(k, plus(at1, 2), at2, 0), ag_r.at[k, 2])
        landed(side(k, plus(at1, 2), at2, 1), ag_r.at[k, 3])
        here = whole(k, plus(at1, 2), at2)
        pass_on(k, 7, second, plus(at2, 1), here)
        pass_on(k, 11, second, plus(at2, 3), here)
        cross(k, 2, 0)

    def ag_second(k, i, j):
        first, second, at1, at2 = line(k)[:4]
        d = (0, 3, 1, 2)[i]
        frm, to = ((3, 1), (1, 3))[j]
        landed(whole(k, plus(at1, d), plus(at2, frm)), ag_r.at[k, 4 + i + 4 * j])
        pass_on(k, 12 + i + 4 * j, second, plus(at2, to), side(k, plus(at1, d), plus(at2, frm), j))
        cross(k, d, frm)

    def ag_last(k, i):
        first, second, at1, at2 = line(k)[:4]
        d = (0, 3, 1, 2)[i]
        landed(side(k, plus(at1, d), plus(at2, 2), 0), ag_r.at[k, 12 + i])
        landed(side(k, plus(at1, d), plus(at2, 2), 1), ag_r.at[k, 16 + i])
        cross(k, d, 2)

    def ag_end(k):
        first, second, at1, at2 = line(k)[:4]
        if crossing(k):
            for d1 in range(4):
                for d2 in range(4):
                    landed(whole(k, plus(at1, d1), plus(at2, d2), 1 - zl), ag_r.at[k, 20 + d1 * 4 + d2])
        landed(whole(k, at1, at2), put_sem.at[k])

    above, below, beyond = plus(h, 1), plus(h, 3), plus(h, 2)
    tall = proj.shape[0] // 2

    def strip(of, who=c):
        return prow.at[:, rows((of * 2 + who) * lanes, lanes)]

    def bit(of, p):
        return prow.at[pl.ds(p * tall, tall), rows((of * 2 + c) * lanes, lanes)]

    def to_core(i, of, src=None):
        send(("p", i), strip(of) if src is None else src, strip(of), p_s.at[i], p_r.at[i], mp_1=1 - c)

    def rows_on():
        take.wait()
        keep.start()
        landed(strip(below), p_r.at[0])
        send(("p", 2), bit(below, 0), bit(below, 0), p_s.at[2], p_r.at[2], mp_0=above)
        landed(strip(above), p_r.at[1])
        send(("p", 3), bit(above, 1), bit(above, 1), p_s.at[3], p_r.at[3], mp_0=below)
        to_core(5, below)
        to_core(6, above)

    def rows_far():
        landed(bit(beyond, 0), p_r.at[2])
        landed(bit(beyond, 1), p_r.at[3])
        to_core(7, beyond)

    def rows_end():
        for i, of in enumerate((h, below, above, beyond)):
            landed(strip(of, 1 - c), p_r.at[4 + i])
        keep.wait()

    take, *state = early
    keep = pltpu.make_async_copy(stage, strip(h), keep_sem)

    def dots(k):
        part[:, cols(k)] = lax.dot_general(
            pa[...], ga[:, cols(k)], (((0,), (0,)), ((), ())), preferred_element_type=f32
        ).astype(part.dtype)

    for cp in state:
        cp.wait()
    steps = {
        "dots": dots, "far": rs_far, "near": rs_near, "turn": rs_turn, "sum": rs_sum, "adam": adam,
        "own": ag_own, "first": ag_first, "farg": ag_far, "second": ag_second, "last": ag_last, "end": ag_end,
        "rows_on": rows_on, "rows_far": rows_far, "rows_end": rows_end,
    }
    for what, *which in ORDER:
        steps[what](*which)
    for cp in sent:
        cp.wait_send()


def split(cols):
    tiles = cols // 128
    widths = [tiles * part // 26 for part in (3, 4, 5, 8)]
    ends = [sum(widths[:k]) for k in range(5)] + [tiles]
    kinds = ((0, False), (1, True), (1, True), (0, False), (1, False))
    return tuple((128 * a, 128 * (b - a), *kind) for a, b, kind in zip(ends, ends[1:], kinds))


def step_kernel(
    chunks, inp, proj, grads, first_in, second_in, weights, new_first, new_second, full, prow, near,
    pa, ga, part, stage, first_m, second_m, early_sem, *rest
):
    y, x, zl, h, c = place()
    peers = [{"mp_1": 1 - c}, {"dp_2": 1 - zl}]
    for axis, at in (("dp_0", y), ("dp_1", x), ("mp_0", h)):
        peers += [{axis: lax.rem(at + 1, 4)}, {axis: lax.rem(at + 3, 4)}]
    peers.append({"dp_0": h, "mp_0": y, "mp_1": 1 - c})
    early = [
        pltpu.make_async_copy(src, dst, early_sem.at[i])
        for i, (src, dst) in enumerate(((proj, stage), (first_in, first_m), (second_in, second_m), (weights, near)))
    ]
    for cp in early:
        cp.start()
    greet(peers, ({"dp_0": h, "mp_0": y}, y != h))
    bufs1, rest = rest[:13], rest[13:]
    sems1, rest = rest[:15], rest[15:]
    bufs2, sems2 = rest[:11], rest[11:]
    p_s, p_r = sems2[-2:]
    lanes = proj.shape[1]
    mine = prow.at[:, rows((h * 2 + c) * lanes, lanes)]
    given = [
        remote(proj, mine, p_s.at[i], p_r.at[i], **where)
        for i, where in (
            (0, {"mp_0": lax.rem(h + 1, 4)}), (1, {"mp_0": lax.rem(h + 3, 4)}), (4, {"mp_1": 1 - c})
        )
    ]

    def rows_own():
        for cp in given:
            cp.start()

    finish = projected_body(inp, proj, grads, pa, ga, *bufs1, rows_own, *sems1)
    update_body(
        chunks, early[:3], pa, ga, proj, new_first, new_second, full, prow,
        part, *bufs2, stage, first_m, second_m, *sems2,
    )
    finish()
    for cp in given:
        cp.wait_send()
    early[3].wait()


def step(inputs, projector, out_grads, first_moment, second_moment, weights):
    tok, feats = inputs.shape
    feat, lanes = projector.shape
    n, cols = first_moment.shape
    bf, f32 = jnp.bfloat16, jnp.float32
    small = pltpu.VMEM((2, tok // 4, lanes), f32)
    slot = pltpu.VMEM((n, cols), bf)
    chunks = split(cols)
    count = len(chunks)
    return pl.pallas_call(
        functools.partial(step_kernel, chunks),
        name="step",
        out_shape=(
            jax.ShapeDtypeStruct((n, cols), f32),
            jax.ShapeDtypeStruct((n, cols), f32),
            jax.ShapeDtypeStruct((32 * n, cols), bf),
            jax.ShapeDtypeStruct((feat, 8 * lanes), bf),
            jax.ShapeDtypeStruct(weights.shape, weights.dtype),
        ),
        in_specs=[ANY] * 6,
        out_specs=(VMEM, VMEM, ANY, ANY, ANY),
        scratch_shapes=[
            pltpu.VMEM((4 * tok, 2 * lanes), bf),
            pltpu.VMEM((4 * tok, cols), bf),
            pltpu.VMEM((8 * n, cols), bf),
            pltpu.VMEM((feat, lanes), bf),
            pltpu.VMEM((n, cols), f32),
            pltpu.VMEM((n, cols), f32),
            DMA((4,)),
            pltpu.VMEM((2, 2 * tok, feats), bf),
            pltpu.VMEM((4 * feat, 2 * lanes), bf),
            pltpu.VMEM((2, 2 * tok, lanes), f32),
            pltpu.VMEM((2, 2 * tok, lanes), f32),
            pltpu.VMEM((2, 2 * tok, lanes), f32),
            *[small] * 8,
            DMA((2,)),
            DMA((6,)), DMA((6,)),
            DMA((6,)), DMA((6,)),
            DMA((1,)), DMA((8,)),
            DMA((8, 3)), DMA((8, 2)),
            DMA((2,)), DMA((2,)),
            DMA((2, 6)), DMA((2, 6)),
            DMA((2, 8)), DMA((2, 8)),
            *[slot] * 10,
            pltpu.VMEM((2 * n, cols), bf),
            DMA,
            DMA((count,)),
            DMA((count, 7)), DMA((count, 7)),
            DMA((count,)), DMA((count,)),
            DMA((count, 36)), DMA((count, 36)),
            DMA((8,)), DMA((8,)),
        ],
        compiler_params=pltpu.CompilerParams(
            collective_id=0, has_side_effects=True, vmem_limit_bytes=24 << 20
        ),
    )(*(in_hbm(v) for v in (inputs, projector, out_grads, first_moment, second_moment, weights)))


def per_device(inputs, projector, out_grads, weights, first_moment, second_moment):
    new_first, new_second, full, ranks, weights = step(
        inputs, projector, out_grads, first_moment, second_moment, weights
    )
    lifted = jnp.dot(ranks, full, preferred_element_type=jnp.float32)
    new_weights = (weights.astype(jnp.float32) - 2.0 * lifted).astype(jnp.bfloat16)
    return (new_weights, new_first, new_second)


def solution(mesh):
    finer = Mesh(mesh.devices.reshape(4, 4, 2, 4, 2), AXES)
    spec = P(DP, MP)
    return jax.shard_map(
        per_device, mesh=finer, in_specs=(spec,) * 6, out_specs=(spec,) * 3, check_vma=False
    )
```

```python
import functools

import jax
import jax.numpy as jnp
from jax import lax
from jax.experimental import pallas as pl
from jax.experimental.pallas import tpu as pltpu
from jax.sharding import Mesh
from jax.sharding import PartitionSpec as P

STEP = 1000
AXES = ("dp_0", "dp_1", "dp_2", "mp_0", "mp_1")
DP = AXES[:3]
MP = AXES[3:]
MESH = pl.DeviceIdType.MESH
ANY = pl.BlockSpec(memory_space=pl.ANY)
VMEM = pl.BlockSpec(memory_space=pltpu.VMEM)
DMA = pltpu.SemaphoreType.DMA


ORDER = (
    ('dots', 0), ('far', 0), ('dots', 1), ('far', 1), ('dots', 2), ('far', 2), ('dots', 3), ('far', 3),
    ('near', 0), ('near', 1), ('near', 2), ('near', 3), ('turn', 0), ('turn', 1), ('turn', 2), ('turn', 3),
    ('sum', 0), ('sum', 1), ('sum', 2), ('adam', 0), ('sum', 3), ('adam', 1), ('rows_on',), ('own', 1),
    ('adam', 2), ('own', 0), ('adam', 3), ('first', 1, 0), ('first', 1, 1), ('second', 1, 0, 0),
    ('second', 1, 0, 1), ('own', 2), ('first', 0, 0), ('own', 3), ('first', 0, 1), ('second', 0, 0, 0),
    ('second', 0, 0, 1), ('farg', 1), ('rows_far',), ('second', 1, 1, 0), ('second', 1, 1, 1),
    ('second', 2, 0, 0), ('second', 1, 2, 0), ('second', 1, 2, 1), ('second', 2, 0, 1), ('last', 1, 0),
    ('second', 0, 1, 0), ('second', 0, 1, 1), ('first', 2, 0), ('first', 2, 1), ('first', 3, 0),
    ('first', 3, 1), ('second', 3, 0, 1), ('farg', 0), ('second', 3, 0, 0), ('second', 0, 2, 0),
    ('second', 0, 2, 1), ('last', 0, 0), ('second', 1, 3, 0), ('second', 1, 3, 1), ('last', 1, 1),
    ('last', 2, 0), ('last', 1, 2), ('last', 0, 1), ('farg', 2), ('second', 2, 1, 0), ('second', 2, 1, 1),
    ('second', 3, 1, 0), ('second', 3, 1, 1), ('second', 2, 2, 0), ('second', 2, 2, 1), ('farg', 3),
    ('second', 3, 2, 0), ('second', 3, 2, 1), ('last', 3, 0), ('last', 1, 3), ('second', 0, 3, 0),
    ('second', 0, 3, 1), ('last', 3, 1), ('last', 0, 2), ('second', 2, 3, 0), ('second', 2, 3, 1),
    ('second', 3, 3, 0), ('second', 3, 3, 1), ('last', 2, 1), ('last', 3, 2), ('last', 2, 2), ('end', 1),
    ('last', 0, 3), ('end', 0), ('last', 3, 3), ('last', 2, 3), ('end', 2), ('end', 3), ('rows_end',),
)


def in_hbm(x):
    return pltpu.with_memory_space_constraint(x, pltpu.HBM)


def place():
    return tuple(lax.axis_index(a) for a in AXES)


def remote(src, dst, send_sem, recv_sem, **where):
    return pltpu.make_async_remote_copy(
        src_ref=src,
        dst_ref=dst,
        send_sem=send_sem,
        recv_sem=recv_sem,
        device_id=where,
        device_id_type=MESH,
    )


def landed(dst, sem):
    pltpu.make_async_copy(dst, dst, sem).wait()


def rows(start, size, unit=None):
    return pl.ds(pl.multiple_of(start, unit or size), size)


def greet(peers, extra=None):
    barrier = pltpu.get_barrier_semaphore()
    for peer in peers:
        pl.semaphore_signal(barrier, inc=1, device_id=peer, device_id_type=MESH)
    count = len(peers)
    if extra is not None:
        peer, present = extra

        @pl.when(present)
        def _():
            pl.semaphore_signal(barrier, inc=1, device_id=peer, device_id_type=MESH)

        count = count + present.astype(jnp.int32)
    pl.semaphore_wait(barrier, count)


def projected_body(
    inp, proj, grads, pa, ga,
    inp4, pq, own, out_half, half_in, via_d, via_u, raw_d, raw_u, turn_u, turn_d, add_d, add_u,
    rows_own, loc_sem, in_s, in_r, g_s, g_r, sw_s, pq_r, ring_s, ring_r, half_s, half_r, rs_s, rs_r, sh_s, sh_r,
):
    y, x, zl, h, c = place()
    up, down = lax.rem(y + 1, 4), lax.rem(y + 3, 4)
    right, left = lax.rem(x + 1, 4), lax.rem(x + 3, 4)
    above, below = lax.rem(h + 1, 4), lax.rem(h + 3, 4)
    tok = inp.shape[0]
    half = tok // 2
    feat, lanes = proj.shape
    wide = ga.shape[1]
    sent = []

    def send(src, dst, s, r, **where):
        cp = remote(src, dst, s, r, **where)
        cp.start()
        sent.append(cp)
        return cp

    core = x // 2

    def block(i, z, k):
        return pq.at[rows((i * 2 + z) * feat, feat), pl.ds(k * lanes, lanes)]

    def part_of(i, z, k, p):
        return pq.at[rows((i * 2 + z) * feat + p * (feat // 2), feat // 2), pl.ds(k * lanes, lanes)]

    spot = pq.at[rows((lax.rem(x, 2) * 2 + zl) * feat, feat), rows(c * lanes, lanes)]
    mark = (lax.rem(x, 2) * 2 + zl) * 2 + c
    at_home = (y == h) & (c == core)
    swap = remote(proj, spot, sw_s.at[0], pq_r.at[mark], dp_0=h, mp_0=y, mp_1=core)
    stay = pltpu.make_async_copy(proj, spot, pq_r.at[mark])

    @pl.when(jnp.logical_not(at_home))
    def _():
        swap.start()

    @pl.when(at_home)
    def _():
        stay.start()

    def slot(k, start, size):
        return inp4.at[k // 2, pl.ds((k % 2) * tok + start, size)]

    lo, hi = pl.ds(0, half), pl.ds(half, half)
    in_up = send(inp.at[lo], slot(1, 0, half), in_s.at[0], in_r.at[0], dp_0=up)
    in_dn = send(inp.at[hi], slot(3, half, half), in_s.at[1], in_r.at[1], dp_0=down)
    in_up2 = send(inp.at[hi], slot(1, half, half), in_s.at[2], in_r.at[2], dp_0=up)
    in_dn2 = send(inp.at[lo], slot(3, 0, half), in_s.at[3], in_r.at[3], dp_0=down)
    own_in = pltpu.make_async_copy(inp, slot(0, 0, tok), loc_sem.at[0])
    own_in.start()
    own_g = pltpu.make_async_copy(grads, ga.at[pl.ds(0, tok)], loc_sem.at[1])
    own_g.start()

    def away(i):
        return lax.rem(x + 4 - (2 * c + i), 4)

    later = []

    def ring(k, dz, stage):
        z = lax.rem(zl + dz, 2)
        for i in range(2):
            m = (i * 2 + z) * 2 + k
            whole = block(i, z, k)
            if stage == 0:
                fr = remote(whole, whole, ring_s.at[m, 0], pq_r.at[m], dp_1=right)
                fl = remote(whole, whole, ring_s.at[m, 1], pq_r.at[m], dp_1=left)
                both = (fr, fl)
                if dz == 0:
                    both = (remote(whole, whole, ring_s.at[m, 2], pq_r.at[m], dp_2=1 - zl), fr, fl)

                @pl.when(away(i) == 0)
                def _():
                    landed(whole, pq_r.at[m])
                    for cp in both:
                        cp.start()

                later.append((away(i) == 0, both))
            if stage == 1:
                for d, p, to in ((1, 0, right), (3, 1, left)):
                    some = part_of(i, z, k, p)
                    fw = remote(some, some, ring_s.at[m, p], ring_r.at[m, p], dp_1=to)

                    @pl.when(away(i) == d)
                    def _():
                        landed(whole, pq_r.at[m])
                        fw.start()

                    later.append((away(i) == d, (fw,)))
            if stage == 2:

                @pl.when(away(i) == 2)
                def _():
                    landed(part_of(i, z, k, 0), ring_r.at[m, 0])
                    landed(part_of(i, z, k, 1), ring_r.at[m, 1])

    ring(0, 0, 0)
    ring(1, 0, 0)
    in_up.wait_recv()
    fw_up = send(slot(1, 0, half), slot(2, 0, half), in_s.at[4], in_r.at[4], dp_0=up)
    in_dn.wait_recv()
    fw_dn = send(slot(3, half, half), slot(2, half, half), in_s.at[5], in_r.at[5], dp_0=down)
    ring(0, 1, 0)
    ring(1, 1, 0)

    def g_from(start, size):
        return ga.at[pl.ds(start, size)]

    g_up = send(grads.at[lo, pl.ds(0, wide)], g_from(tok, half), g_s.at[0], g_r.at[0], dp_0=up)
    g_dn = send(grads.at[hi, pl.ds(0, wide)], g_from(3 * tok + half, half), g_s.at[1], g_r.at[1], dp_0=down)
    g_up2 = send(grads.at[hi, pl.ds(0, wide)], g_from(tok + half, half), g_s.at[2], g_r.at[2], dp_0=up)
    g_dn2 = send(grads.at[lo, pl.ds(0, wide)], g_from(3 * tok, half), g_s.at[3], g_r.at[3], dp_0=down)
    for k in range(2):
        for dz in range(2):
            ring(k, dz, 1)
    own_in.wait()
    in_up2.wait_recv()
    in_dn2.wait_recv()
    fw_up.wait_recv()
    fw_dn.wait_recv()

    pairs = []
    for k in range(2):
        for dz in range(2):
            ring(k, dz, 2)
        out_half[k] = jnp.dot(
            inp4[1 - c], pq[:, pl.ds(k * lanes, lanes)], preferred_element_type=jnp.float32
        )
        pairs.append(send(out_half.at[k], half_in.at[k], half_s.at[k], half_r.at[k], mp_1=1 - c))
    for k in range(2):
        own[k] = jnp.dot(inp4[c], pq[:, pl.ds(k * lanes, lanes)], preferred_element_type=jnp.float32)

    cut = 2 * tok // 4
    q = cut // 2
    beyond = lax.rem(h + 2, 4)
    flow = {}

    def piece(k, of, p):
        return own.at[k, rows(of * cut + p * q, q)]

    def value(k, of, p):
        return own[k, rows(of * cut + p * q, q)]

    for k in range(2):
        pairs[k].wait_recv()
        own[k] += half_in[k]
        flow[k, 0] = send(piece(k, beyond, 0), via_d.at[k], rs_s.at[k, 0], rs_r.at[k, 0], mp_0=above)
        flow[k, 1] = send(piece(k, beyond, 1), via_u.at[k], rs_s.at[k, 1], rs_r.at[k, 1], mp_0=below)
        flow[k, 2] = send(piece(k, above, 1), raw_d.at[k], rs_s.at[k, 2], rs_r.at[k, 2], mp_0=above)
        flow[k, 3] = send(piece(k, below, 0), raw_u.at[k], rs_s.at[k, 3], rs_r.at[k, 3], mp_0=below)
    for k in range(2):
        flow[k, 0].wait_recv()
        turn_u[k] = via_d[k] + value(k, above, 0)
        flow[k, 4] = send(turn_u.at[k], add_d.at[k], rs_s.at[k, 4], rs_r.at[k, 4], mp_0=above)
        flow[k, 1].wait_recv()
        turn_d[k] = via_u[k] + value(k, below, 1)
        flow[k, 5] = send(turn_d.at[k], add_u.at[k], rs_s.at[k, 5], rs_r.at[k, 5], mp_0=below)

    def share(k, of, start=0, size=cut, who=c):
        return pa.at[rows(who * 2 * tok + of * cut + start, size, size), pl.ds(k * lanes, lanes)]

    for k in range(2):
        for i in (2, 3, 4, 5):
            flow[k, i].wait_recv()
        top = value(k, h, 0) + add_d[k] + raw_u[k]
        low = value(k, h, 1) + add_u[k] + raw_d[k]
        pa[rows(c * 2 * tok + h * cut, cut), pl.ds(k * lanes, lanes)] = jnp.concatenate(
            [top, low], axis=0
        ).astype(pa.dtype)
        flow[k, 6] = send(share(k, h), share(k, h), sh_s.at[k, 0], sh_r.at[k, 0], mp_0=above)
        flow[k, 7] = send(share(k, h), share(k, h), sh_s.at[k, 1], sh_r.at[k, 1], mp_0=below)
        send(share(k, h), share(k, h), sh_s.at[k, 4], sh_r.at[k, 4], mp_1=1 - c)
    g_up.wait_recv()
    gf_up = send(g_from(tok, half), g_from(2 * tok, half), g_s.at[4], g_r.at[4], dp_0=up)
    g_dn.wait_recv()
    gf_dn = send(
        g_from(3 * tok + half, half), g_from(2 * tok + half, half), g_s.at[5], g_r.at[5], dp_0=down
    )
    for k in range(2):
        landed(share(k, below), sh_r.at[k, 0])
        send(share(k, below, 0, q), share(k, below, 0, q), sh_s.at[k, 2], sh_r.at[k, 2], mp_0=above)
        send(share(k, below), share(k, below), sh_s.at[k, 5], sh_r.at[k, 5], mp_1=1 - c)
        landed(share(k, above), sh_r.at[k, 1])
        send(share(k, above, q, q), share(k, above, q, q), sh_s.at[k, 3], sh_r.at[k, 3], mp_0=below)
        send(share(k, above), share(k, above), sh_s.at[k, 6], sh_r.at[k, 6], mp_1=1 - c)
    for k in range(2):
        landed(share(k, beyond, 0, q), sh_r.at[k, 2])
        landed(share(k, beyond, q, q), sh_r.at[k, 3])
        send(share(k, beyond), share(k, beyond), sh_s.at[k, 7], sh_r.at[k, 7], mp_1=1 - c)
    rows_own()
    for k in range(2):
        for i, of in enumerate((h, below, above, beyond)):
            landed(share(k, of, who=1 - c), sh_r.at[k, 4 + i])
    g_up2.wait_recv()
    g_dn2.wait_recv()
    gf_up.wait_recv()
    gf_dn.wait_recv()
    own_g.wait()

    def finish():
        for cp in sent:
            cp.wait_send()
        for when, copies in later + [(jnp.logical_not(at_home), (swap,))]:

            @pl.when(when)
            def _():
                for cp in copies:
                    cp.wait_send()

    return finish


def update_body(
    chunks, early, pa, ga, proj, new_first, new_second, full, prow,
    part, raw_l, raw_r, via_l, via_r, turn_r, turn_l, add_l, add_r, zsend, zrecv, both, stage, first_m, second_m,
    keep_sem, put_sem, rs_s, rs_r, d_s, d_r, ag_s, ag_r, p_s, p_r,
):
    y, x, zl, h, c = place()
    n = first_m.shape[0]
    lanes = proj.shape[1]
    f32 = jnp.float32
    right, left, far = lax.rem(x + 1, 4), lax.rem(x + 3, 4), lax.rem(x + 2, 4)

    def plus(at, d):
        return lax.rem(at + d, 4)

    sent = []
    flow = {}

    def send(name, src, dst, s, r, **where):
        cp = remote(src, dst, s, r, **where)
        cp.start()
        sent.append(cp)
        flow[name] = cp

    def cols(k):
        return pl.ds(chunks[k][0], chunks[k][1])

    def piece(k, of, half):
        return part.at[rows(of * 2 * n + half * n, n), cols(k)]

    def mine_of(k, start):
        return part[rows(start, n), cols(k)].astype(f32)

    def at(ref, k):
        return ref.at[:, cols(k)]

    def rs_far(k):
        send((k, 0), piece(k, far, 0), at(via_l, k), rs_s.at[k, 0], rs_r.at[k, 0], dp_1=right)
        send((k, 1), piece(k, far, 1), at(via_r, k), rs_s.at[k, 1], rs_r.at[k, 1], dp_1=left)

    def rs_near(k):
        send((k, 2), piece(k, right, 1), at(raw_l, k), rs_s.at[k, 2], rs_r.at[k, 2], dp_1=right)
        send((k, 3), piece(k, left, 0), at(raw_r, k), rs_s.at[k, 3], rs_r.at[k, 3], dp_1=left)

    def load(ref, k, where=slice(None)):
        return ref[where, cols(k)].astype(f32)

    def rs_turn(k):
        flow[k, 0].wait_recv()
        turn_r[:, cols(k)] = (load(via_l, k) + mine_of(k, right * 2 * n)).astype(turn_r.dtype)
        send((k, 4), at(turn_r, k), at(add_l, k), rs_s.at[k, 4], rs_r.at[k, 4], dp_1=right)
        flow[k, 1].wait_recv()
        turn_l[:, cols(k)] = (load(via_r, k) + mine_of(k, left * 2 * n + n)).astype(turn_l.dtype)
        send((k, 5), at(turn_l, k), at(add_r, k), rs_s.at[k, 5], rs_r.at[k, 5], dp_1=left)

    def total(k, half):
        if half == 0:
            return mine_of(k, x * 2 * n) + load(add_l, k) + load(raw_r, k)
        return mine_of(k, x * 2 * n + n) + load(add_r, k) + load(raw_l, k)

    def rs_sum(k):
        for i in (2, 3, 4, 5):
            flow[k, i].wait_recv()
        for mine in range(2):

            @pl.when(zl == mine)
            def _():
                zsend[:, cols(k)] = total(k, 1 - mine).astype(zsend.dtype)

        send((k, 6), at(zsend, k), at(zrecv, k), rs_s.at[k, 6], rs_r.at[k, 6], dp_2=1 - zl)
        for mine in range(2):

            @pl.when(zl == mine)
            def _():
                new_first[:, cols(k)] = total(k, mine)

    def adam(k):
        flow[k, 6].wait_recv()
        grad = new_first[:, cols(k)] + load(zrecv, k)
        m1 = 0.9 * first_m[:, cols(k)] + 0.1 * grad
        m2 = 0.999 * second_m[:, cols(k)] + 0.001 * grad * grad
        new_first[:, cols(k)] = m1
        new_second[:, cols(k)] = m2
        first_fix = 1.0 - 0.9**STEP
        second_fix = 1.0 - 0.999**STEP
        both[rows(zl * n, n), cols(k)] = (
            m1 / first_fix / (jnp.sqrt(m2 / second_fix) + 1e-08)
        ).astype(both.dtype)
        own = both.at[rows(zl * n, n), cols(k)]
        if not crossing(k):
            send((k, "d"), own, own, d_s.at[k], d_r.at[k], dp_2=1 - zl)

    def crossing(k):
        return chunks[k][3]

    def line(k):
        if chunks[k][2] == 0:
            return "dp_1", "dp_0", x, y, 1, 4
        return "dp_0", "dp_1", y, x, 4, 1

    def deep(k):
        return n if crossing(k) else 2 * n

    def region(k, p1, p2, start, size, z=zl):
        f1, f2 = line(k)[4:]
        if crossing(k):
            start = start + z * n
        return full.at[rows((p1 * f1 + p2 * f2) * 2 * n + start, size, n // 2), cols(k)]

    def whole(k, p1, p2, z=zl):
        return region(k, p1, p2, 0, deep(k), z)

    def side(k, p1, p2, half):
        size = deep(k) // 2
        return region(k, p1, p2, half * size, size)

    def pass_on(k, i, axis, to, where, src=None):
        send((k, "a", i), where if src is None else src, where, ag_s.at[k, i], ag_r.at[k, i], **{axis: to})

    def cross(k, d1, d2, src=None):
        if crossing(k):
            at1, at2 = line(k)[2:4]
            where, i = whole(k, plus(at1, d1), plus(at2, d2)), 20 + d1 * 4 + d2
            send((k, "a", i), where if src is None else src, where, ag_s.at[k, i], ag_r.at[k, i], dp_2=1 - zl)

    def ag_own(k):
        first, second, at1, at2 = line(k)[:4]
        if crossing(k):
            src = both.at[rows(zl * n, n), cols(k)]
        else:
            landed(both.at[rows((1 - zl) * n, n), cols(k)], d_r.at[k])
            src = both.at[:, cols(k)]
        here = whole(k, at1, at2)
        pass_on(k, 0, first, plus(at1, 1), here, src)
        pass_on(k, 1, first, plus(at1, 3), here, src)
        pass_on(k, 4, second, plus(at2, 1), here, src)
        pass_on(k, 8, second, plus(at2, 3), here, src)
        cross(k, 0, 0, src)
        pltpu.make_async_copy(src, here, put_sem.at[k]).start()

    def ag_first(k, j):
        first, second, at1, at2 = line(k)[:4]
        d, to = ((3, 1), (1, 3))[j]
        here = whole(k, plus(at1, d), at2)
        landed(here, ag_r.at[k, j])
        pass_on(k, 2 + j, first, plus(at1, to), side(k, plus(at1, d), at2, j))
        pass_on(k, 5 + j, second, plus(at2, 1), here)
        pass_on(k, 9 + j, second, plus(at2, 3), here)
        cross(k, d, 0)

    def ag_far(k):
        first, second, at1, at2 = line(k)[:4]
        landed(side(k, plus(at1, 2), at2, 0), ag_r.at[k, 2])
        landed(side(k, plus(at1, 2), at2, 1), ag_r.at[k, 3])
        here = whole(k, plus(at1, 2), at2)
        pass_on(k, 7, second, plus(at2, 1), here)
        pass_on(k, 11, second, plus(at2, 3), here)
        cross(k, 2, 0)

    def ag_second(k, i, j):
        first, second, at1, at2 = line(k)[:4]
        d = (0, 3, 1, 2)[i]
        frm, to = ((3, 1), (1, 3))[j]
        landed(whole(k, plus(at1, d), plus(at2, frm)), ag_r.at[k, 4 + i + 4 * j])
        pass_on(k, 12 + i + 4 * j, second, plus(at2, to), side(k, plus(at1, d), plus(at2, frm), j))
        cross(k, d, frm)

    def ag_last(k, i):
        first, second, at1, at2 = line(k)[:4]
        d = (0, 3, 1, 2)[i]
        landed(side(k, plus(at1, d), plus(at2, 2), 0), ag_r.at[k, 12 + i])
        landed(side(k, plus(at1, d), plus(at2, 2), 1), ag_r.at[k, 16 + i])
        cross(k, d, 2)

    def ag_end(k):
        first, second, at1, at2 = line(k)[:4]
        if crossing(k):
            for d1 in range(4):
                for d2 in range(4):
                    landed(whole(k, plus(at1, d1), plus(at2, d2), 1 - zl), ag_r.at[k, 20 + d1 * 4 + d2])
        landed(whole(k, at1, at2), put_sem.at[k])

    above, below, beyond = plus(h, 1), plus(h, 3), plus(h, 2)
    tall = proj.shape[0] // 2

    def strip(of, who=c):
        return prow.at[:, rows((of * 2 + who) * lanes, lanes)]

    def bit(of, p):
        return prow.at[pl.ds(p * tall, tall), rows((of * 2 + c) * lanes, lanes)]

    def to_core(i, of, src=None):
        send(("p", i), strip(of) if src is None else src, strip(of), p_s.at[i], p_r.at[i], mp_1=1 - c)

    def rows_on():
        take.wait()
        keep.start()
        landed(strip(below), p_r.at[0])
        send(("p", 2), bit(below, 0), bit(below, 0), p_s.at[2], p_r.at[2], mp_0=above)
        landed(strip(above), p_r.at[1])
        send(("p", 3), bit(above, 1), bit(above, 1), p_s.at[3], p_r.at[3], mp_0=below)
        to_core(5, below)
        to_core(6, above)

    def rows_far():
        landed(bit(beyond, 0), p_r.at[2])
        landed(bit(beyond, 1), p_r.at[3])
        to_core(7, beyond)

    def rows_end():
        for i, of in enumerate((h, below, above, beyond)):
            landed(strip(of, 1 - c), p_r.at[4 + i])
        keep.wait()

    take, *state = early
    keep = pltpu.make_async_copy(stage, strip(h), keep_sem)

    def dots(k):
        part[:, cols(k)] = lax.dot_general(
            pa[...], ga[:, cols(k)], (((0,), (0,)), ((), ())), preferred_element_type=f32
        ).astype(part.dtype)

    for cp in state:
        cp.wait()
    steps = {
        "dots": dots, "far": rs_far, "near": rs_near, "turn": rs_turn, "sum": rs_sum, "adam": adam,
        "own": ag_own, "first": ag_first, "farg": ag_far, "second": ag_second, "last": ag_last, "end": ag_end,
        "rows_on": rows_on, "rows_far": rows_far, "rows_end": rows_end,
    }
    for what, *which in ORDER:
        steps[what](*which)
    for cp in sent:
        cp.wait_send()


def split(cols):
    tiles = cols // 128
    widths = [tiles * part // 26 for part in (6, 9, 5)]
    ends = [sum(widths[:k]) for k in range(4)] + [tiles]
    kinds = ((0, False), (1, True), (0, False), (1, False))
    return tuple((128 * a, 128 * (b - a), *kind) for a, b, kind in zip(ends, ends[1:], kinds))


def step_kernel(
    chunks, inp, proj, grads, first_in, second_in, weights, new_first, new_second, full, prow, near,
    pa, ga, part, stage, first_m, second_m, early_sem, *rest
):
    y, x, zl, h, c = place()
    peers = [{"mp_1": 1 - c}, {"dp_2": 1 - zl}]
    for axis, at in (("dp_0", y), ("dp_1", x), ("mp_0", h)):
        peers += [{axis: lax.rem(at + 1, 4)}, {axis: lax.rem(at + 3, 4)}]
    peers.append({"dp_0": h, "mp_0": y, "mp_1": 1 - c})
    early = [
        pltpu.make_async_copy(src, dst, early_sem.at[i])
        for i, (src, dst) in enumerate(((proj, stage), (first_in, first_m), (second_in, second_m), (weights, near)))
    ]
    for cp in early:
        cp.start()
    greet(peers, ({"dp_0": h, "mp_0": y}, y != h))
    bufs1, rest = rest[:13], rest[13:]
    sems1, rest = rest[:15], rest[15:]
    bufs2, sems2 = rest[:11], rest[11:]
    p_s, p_r = sems2[-2:]
    lanes = proj.shape[1]
    mine = prow.at[:, rows((h * 2 + c) * lanes, lanes)]
    given = [
        remote(proj, mine, p_s.at[i], p_r.at[i], **where)
        for i, where in (
            (0, {"mp_0": lax.rem(h + 1, 4)}), (1, {"mp_0": lax.rem(h + 3, 4)}), (4, {"mp_1": 1 - c})
        )
    ]

    def rows_own():
        for cp in given:
            cp.start()

    finish = projected_body(inp, proj, grads, pa, ga, *bufs1, rows_own, *sems1)
    update_body(
        chunks, early[:3], pa, ga, proj, new_first, new_second, full, prow,
        part, *bufs2, stage, first_m, second_m, *sems2,
    )
    finish()
    for cp in given:
        cp.wait_send()
    early[3].wait()


def step(inputs, projector, out_grads, first_moment, second_moment, weights):
    tok, feats = inputs.shape
    feat, lanes = projector.shape
    n, cols = first_moment.shape
    bf, f32 = jnp.bfloat16, jnp.float32
    small = pltpu.VMEM((2, tok // 4, lanes), f32)
    slot = pltpu.VMEM((n, cols), bf)
    chunks = split(cols)
    count = len(chunks)
    return pl.pallas_call(
        functools.partial(step_kernel, chunks),
        name="step",
        out_shape=(
            jax.ShapeDtypeStruct((n, cols), f32),
            jax.ShapeDtypeStruct((n, cols), f32),
            jax.ShapeDtypeStruct((32 * n, cols), bf),
            jax.ShapeDtypeStruct((feat, 8 * lanes), bf),
            jax.ShapeDtypeStruct(weights.shape, weights.dtype),
        ),
        in_specs=[ANY] * 6,
        out_specs=(VMEM, VMEM, ANY, ANY, ANY),
        scratch_shapes=[
            pltpu.VMEM((4 * tok, 2 * lanes), bf),
            pltpu.VMEM((4 * tok, cols), bf),
            pltpu.VMEM((8 * n, cols), bf),
            pltpu.VMEM((feat, lanes), bf),
            pltpu.VMEM((n, cols), f32),
            pltpu.VMEM((n, cols), f32),
            DMA((4,)),
            pltpu.VMEM((2, 2 * tok, feats), bf),
            pltpu.VMEM((4 * feat, 2 * lanes), bf),
            pltpu.VMEM((2, 2 * tok, lanes), f32),
            pltpu.VMEM((2, 2 * tok, lanes), f32),
            pltpu.VMEM((2, 2 * tok, lanes), f32),
            *[small] * 8,
            DMA((2,)),
            DMA((6,)), DMA((6,)),
            DMA((6,)), DMA((6,)),
            DMA((1,)), DMA((8,)),
            DMA((8, 3)), DMA((8, 2)),
            DMA((2,)), DMA((2,)),
            DMA((2, 6)), DMA((2, 6)),
            DMA((2, 8)), DMA((2, 8)),
            *[slot] * 10,
            pltpu.VMEM((2 * n, cols), bf),
            DMA,
            DMA((count,)),
            DMA((count, 7)), DMA((count, 7)),
            DMA((count,)), DMA((count,)),
            DMA((count, 36)), DMA((count, 36)),
            DMA((8,)), DMA((8,)),
        ],
        compiler_params=pltpu.CompilerParams(
            collective_id=0, has_side_effects=True, vmem_limit_bytes=24 << 20
        ),
    )(*(in_hbm(v) for v in (inputs, projector, out_grads, first_moment, second_moment, weights)))


def per_device(inputs, projector, out_grads, weights, first_moment, second_moment):
    new_first, new_second, full, ranks, weights = step(
        inputs, projector, out_grads, first_moment, second_moment, weights
    )
    lifted = jnp.dot(ranks, full, preferred_element_type=jnp.float32)
    new_weights = (weights.astype(jnp.float32) - 2.0 * lifted).astype(jnp.bfloat16)
    return (new_weights, new_first, new_second)


def solution(mesh):
    finer = Mesh(mesh.devices.reshape(4, 4, 2, 4, 2), AXES)
    spec = P(DP, MP)
    return jax.shard_map(
        per_device, mesh=finer, in_specs=(spec,) * 6, out_specs=(spec,) * 3, check_vma=False
    )
```
